32 devices in a mesh: ctx: 8 (over z, x), chan: 2 (over core), dp: 2 (over y).
Axes of the slice: x: 2, y: 2, z: 4, core: 2. Of those that a mesh axis runs over, the one named last changes fastest.
Arguments:
- q_stream: bfloat16 [2, 2048, 4096], P('dp', 'ctx', 'chan'), may hold values from -6 to 6
- k_stream: bfloat16 [2, 2048, 4096], P('dp', 'ctx', 'chan'), may hold values from -6 to 6
- v_stream: bfloat16 [2, 2048, 4096], P('dp', 'ctx', 'chan'), may hold values from -6 to 6
- out_grad: bfloat16 [2, 2048, 4096], P('dp', 'ctx', 'chan'), may hold values from -6 to 6
- norm_gain: float32 [4096], P('chan'), may hold values from 0.1 to 1.9
- residue: float32 [4096, 16], P('chan'), may hold values from -6 to 6
- rate: float32 [4096, 16], P('chan'), may hold values from -1.5 to 6
Outputs:
- y_out: bfloat16 [2, 2048, 4096], P('dp', 'ctx', 'chan')
- grad_q: bfloat16 [2, 2048, 4096], P('dp', 'ctx', 'chan')
- grad_k: bfloat16 [2, 2048, 4096], P('dp', 'ctx', 'chan')
- grad_v: bfloat16 [2, 2048, 4096], P('dp', 'ctx', 'chan')
- grad_residue: float32 [4096, 16], P('chan')
- grad_rate: float32 [4096, 16], P('chan')
- grad_gain: float32 [4096], P('chan')
The draws below stay inside these ranges and needn't reach their ends.
All inputs are finite; a program needn't handle non-finite values.
Results may differ from the reference program's by a relative error of at most 0.0051.
Values may be sent and summed in bfloat16 or wider, within the bound.
No kernel may reach another device: no remote copies, remote signals or barrier semaphores. Data moves between devices by JAX's collectives and lax.ppermute only.
A program may use at most 128 MiB of HBM per device.

```python
import jax
import jax.numpy as jnp
from jax import lax

D = 4096
MODES = 16
SEQ = 2048
BATCH = 2


def block_levels(rng, dims, shards, smallest, high):
    loudness = 1.0
    for position, parts in shards:
        heights = jax.random.uniform(jax.random.fold_in(jax.random.fold_in(rng, 6), position), (parts,), jnp.float32, smallest / len(shards), high / len(shards))
        loudness = loudness * jnp.repeat(jnp.exp(heights), dims[position] // parts).reshape((-1,) + (1,) * (len(dims) - 1 - position))
    return loudness


def scatter_about(stream_key, extent, scale, bound, split=(), held_as=jnp.bfloat16):
    entries = scale * jax.random.normal(stream_key, extent, jnp.float32)
    if split:
        entries = entries * block_levels(stream_key, extent, split, -0.22, 0.18)
    return jnp.clip(entries, -bound, bound).astype(held_as)


def setup_inputs(seed: int = 0) -> dict:
    seeds = jax.random.split(jax.random.key(seed), 8)
    q_stream = scatter_about(seeds[0], (BATCH, SEQ, D), 1.0, 6.0, ((0, 2), (1, 8), (2, 2)))
    k_stream = scatter_about(seeds[1], (BATCH, SEQ, D), 1.0, 6.0, ((0, 2), (1, 8), (2, 2)))
    v_stream = scatter_about(seeds[2], (BATCH, SEQ, D), 1.0, 6.0, ((0, 2), (1, 8), (2, 2)))
    out_grad = scatter_about(seeds[3], (BATCH, SEQ, D), 1.0, 6.0, ((0, 2), (1, 8), (2, 2)))
    norm_gain = jnp.clip(1.0 + 0.18 * jax.random.normal(seeds[4], (D,), jnp.float32), 0.1, 1.9)
    residue = scatter_about(seeds[5], (D, MODES), 1.0, 6.0, ((0, 2),), jnp.float32)
    rate = jnp.clip(-1.5 + 7.5 * jax.random.uniform(seeds[6], (D, MODES), jnp.float32) ** block_levels(seeds[6], (D, MODES), ((0, 2),), -0.2, 0.2), -1.5, 6.0)
    return {"q_stream": q_stream, "k_stream": k_stream, "v_stream": v_stream, "out_grad": out_grad, "norm_gain": norm_gain, "residue": residue, "rate": rate}


epsilon = 1e-06

def gating(conv, q_part, grad_part, norm_gain):
    q_float = q_part.astype(jnp.float32)
    grad_float = grad_part.astype(jnp.float32)
    mixed = q_float * conv
    scaled = norm_gain * grad_float
    squares = lax.optimization_barrier(jnp.sum(mixed * mixed, axis=-1))
    inner_sum = lax.optimization_barrier(jnp.sum(scaled * mixed, axis=-1))
    inv_rms = lax.rsqrt(squares / D + epsilon)[..., None]
    inner_sum = inner_sum[..., None]
    y_part = (norm_gain * mixed * inv_rms).astype(jnp.bfloat16)
    mixed_grad = inv_rms * scaled - mixed * (inv_rms * inv_rms * inv_rms * inner_sum / D)
    grad_q = (mixed_grad * conv).astype(jnp.bfloat16)
    gate_grad = mixed_grad * q_float
    gain_part = lax.optimization_barrier(jnp.sum(grad_float * mixed * inv_rms, axis=0))
    return (y_part, grad_q, gate_grad, gain_part)

def reference(q_stream, k_stream, v_stream, out_grad, norm_gain, residue, rate):
    seq_len = q_stream.shape[1]
    period = 2 * seq_len
    channels = q_stream.shape[2]
    values = (k_stream.astype(jnp.float32) * v_stream.astype(jnp.float32)).astype(jnp.bfloat16)
    values = lax.optimization_barrier(values).astype(jnp.float32)
    decays = jnp.exp(rate) / seq_len
    offsets = jnp.arange(seq_len, dtype=jnp.float32)
    kernel = jnp.zeros((seq_len, channels), jnp.float32)
    for mode in range(MODES):
        kernel = kernel + residue[:, mode] * jnp.exp(-offsets[:, None] * decays[:, mode])
    kernel_f = jnp.fft.rfft(kernel, n=period, axis=0)
    cross_f = jnp.zeros_like(kernel_f)
    y_rows, gq_rows, gk_rows, gv_rows = ([], [], [], [])
    gain_total = jnp.zeros((channels,), jnp.float32)
    for row in range(q_stream.shape[0]):
        value_f = jnp.fft.rfft(values[row], n=period, axis=0)
        conv = jnp.fft.irfft(value_f * kernel_f, n=period, axis=0)[:seq_len]
        y_part, grad_q, gate_grad, gain_part = gating(conv, q_stream[row], out_grad[row], norm_gain)
        gate_f = jnp.fft.rfft(gate_grad, n=period, axis=0)
        value_grad = jnp.fft.irfft(gate_f * jnp.conj(kernel_f), n=period, axis=0)[:seq_len]
        cross_f = cross_f + gate_f * jnp.conj(value_f)
        y_rows.append(y_part)
        gq_rows.append(grad_q)
        gk_rows.append((value_grad * v_stream[row].astype(jnp.float32)).astype(jnp.bfloat16))
        gv_rows.append((value_grad * k_stream[row].astype(jnp.float32)).astype(jnp.bfloat16))
        gain_total = gain_total + gain_part
    kernel_grad = jnp.fft.irfft(cross_f, n=period, axis=0)[:seq_len]
    res_cols, rate_cols = ([], [])
    for mode in range(MODES):
        weights = jnp.exp(-offsets[:, None] * decays[:, mode])
        res_cols.append(lax.optimization_barrier(jnp.sum(kernel_grad * weights, axis=0)))
        rate_cols.append(-decays[:, mode] * residue[:, mode] * lax.optimization_barrier(jnp.sum(kernel_grad * offsets[:, None] * weights, axis=0)))
    return (jnp.stack(y_rows, 0), jnp.stack(gq_rows, 0), jnp.stack(gk_rows, 0), jnp.stack(gv_rows, 0), jnp.stack(res_cols, 1), jnp.stack(rate_cols, 1), gain_total)
```

```python
import functools

import jax
import jax.numpy as jnp
import numpy as np
from jax import lax
from jax.experimental import pallas as pl
from jax.experimental.pallas import tpu as pltpu
from jax.sharding import PartitionSpec as P

EPSILON = 1e-06
LANES = 128
ROWS = 8
F32 = jnp.float32
BF16 = jnp.bfloat16
VMEM_LIMIT = 40 * 1024 * 1024


def fourier(length):
    freq = 2 * np.arange(length)[:, None] + 1
    phase = (freq * np.arange(length)[None, :]) % (4 * length) * (2.0 * np.pi / (4 * length))
    full = np.concatenate([np.cos(phase), -np.sin(phase)], axis=0).astype(np.float32)
    return full


def halves(full):
    high = full.astype(jnp.bfloat16)
    low = (full - high.astype(np.float32)).astype(jnp.bfloat16)
    return jnp.asarray(high), jnp.asarray(low)


def split(x):
    high = x.astype(BF16)
    return high, (x - high.astype(F32)).astype(BF16)


def dot(a, b):
    return jnp.dot(a, b, preferred_element_type=F32)


def dot3(a_high, a_low, x):
    high, low = split(x)
    return dot(a_high, high) + (dot(a_high, low) + dot(a_low, high))


def spread(ref, cols):
    return jnp.stack(
        [jnp.broadcast_to(ref[m : m + 1, cols], (ROWS, LANES)) for m in range(ref.shape[0])]
    )


def sublane():
    return lax.broadcasted_iota(jnp.int32, (1, ROWS, LANES), 1).astype(F32)


def group(i):
    return pl.ds(pl.multiple_of(i * LANES, LANES), LANES)


def evaluate(start, step, tiles):
    term = start
    for i in range(tiles):
        yield jnp.sum(term, axis=0)
        if i + 1 < tiles:
            term = term * step


def combine(pieces, decay_block, gap):
    total = pieces[-1]
    slope = jnp.zeros_like(total)
    for piece in pieces[-2::-1]:
        slope = decay_block * (slope + total)
        total = piece + decay_block * total
    return total, slope * gap


def state_kernel(k_ref, v_ref, lam_ref, val_ref, s_ref):
    length, width = k_ref.shape

    def body(i, _):
        cols = group(i)
        lam = spread(lam_ref, cols)
        step = jnp.exp(-ROWS * lam)
        acc = jnp.zeros_like(lam)
        for a in range(0, length, 16):
            vals = (k_ref[a : a + 16, cols].astype(F32) * v_ref[a : a + 16, cols].astype(F32)).astype(BF16)
            val_ref[a : a + 16, cols] = vals
            vals = vals.astype(F32)
            acc = acc * step + vals[None, :ROWS]
            acc = acc * step + vals[None, ROWS:]
        weight = jnp.exp(-lam * (ROWS - 1 - sublane()))
        s_ref[:, cols] = jnp.sum(acc * weight, axis=1).astype(s_ref.dtype)
        return 0

    lax.fori_loop(0, width // LANES, body, 0)


def local_kernel(val_ref, lam_ref, res_ref, fh_ref, fl_ref, th_ref, tl_ref,
                 conv_ref, vs_ref, ks_ref, slope_ref, ker):
    length, width = val_ref.shape
    tiles = length // ROWS

    def body(i, _):
        cols = group(i)
        lam = spread(lam_ref, cols)
        step = jnp.exp(-ROWS * lam)
        start = spread(res_ref, cols) * jnp.exp(-lam * sublane())
        for a, tile in enumerate(evaluate(start, step, tiles)):
            ker[a * ROWS : (a + 1) * ROWS, cols] = tile
        acc = jnp.zeros_like(lam)
        for a in range(0, length, 16):
            vals = val_ref[a : a + 16, cols].astype(F32)
            for h in (0, ROWS):
                away = (length - 1 - a - h) - sublane()[0]
                acc = acc * step + (vals[h : h + ROWS] * away)[None]
        weight = jnp.exp(-lam * (ROWS - 1 - sublane()))
        slope_ref[:, cols] = jnp.sum(acc * weight, axis=1).astype(slope_ref.dtype)
        return 0

    lax.fori_loop(0, width // LANES, body, 0)
    vals = val_ref[...]
    vs = dot(fh_ref[...], vals) + dot(fl_ref[...], vals)
    vs_ref[...] = vs
    ks = dot3(fh_ref[...], fl_ref[...], ker[...])
    ks_ref[...] = ks
    vr, vi = vs[:length], vs[length:]
    kr, ki = ks[:length], ks[length:]
    prod = jnp.concatenate([vr * kr - vi * ki, vr * ki + vi * kr], axis=0) * (1.0 / length)
    conv_ref[...] = dot3(th_ref[...], tl_ref[...], prod)


def forward_kernel(n_in, length_gap, *refs):
    pieces, (lam_ref, res_ref, conv_in_ref, q_ref, og_ref, gain_ref,
             conv_ref, sums_ref, state_ref, held) = refs[:n_in], refs[n_in:]
    length, width = q_ref.shape

    @pl.when(pl.program_id(0) == 0)
    def _():
        sums_ref[...] = jnp.zeros_like(sums_ref)

    def body(i, _):
        cols = group(i)
        decay_block = jnp.exp(-length_gap * lam_ref[:, cols])
        total, _ = combine([p[:, cols].astype(F32) for p in pieces], decay_block, length_gap)
        state_ref[:, cols] = total
        held[...] = total * res_ref[:, cols]
        lam = spread(lam_ref, cols)
        step = jnp.exp(-ROWS * lam)
        start = spread(held, slice(None)) * jnp.exp(-lam * (sublane() + 1.0))
        gain = gain_ref[:, cols]
        tiles = evaluate(start, step, length // ROWS)
        for a in range(0, length, 16):
            rows = slice(a, a + 16)
            conv = conv_in_ref[rows, cols] + jnp.concatenate([next(tiles), next(tiles)], axis=0)
            conv_ref[rows, cols] = conv
            mixed = q_ref[rows, cols].astype(F32) * conv
            scaled = gain * og_ref[rows, cols].astype(F32)
            sums_ref[0, rows] += mixed * mixed
            sums_ref[1, rows] += scaled * mixed
        return 0

    lax.fori_loop(0, width // LANES, body, 0)


def gate_kernel(model_width, sums_ref, peer_ref, lam_ref, conv_ref, q_ref, og_ref, gain_ref,
                y_ref, gq_ref, gate_ref, gain_part_ref, gw_ref, inv_ref, coef_ref):
    length, width = q_ref.shape

    @pl.when(pl.program_id(0) == 0)
    def _():
        squares = jnp.sum(sums_ref[0] + peer_ref[0], axis=1, keepdims=True)
        inner = jnp.sum(sums_ref[1] + peer_ref[1], axis=1, keepdims=True)
        inv = lax.rsqrt(squares / model_width + EPSILON)
        coef = inv * inv * inv * inner / model_width
        inv_ref[...] = jnp.broadcast_to(inv, inv_ref.shape)
        coef_ref[...] = jnp.broadcast_to(coef, coef_ref.shape)

    def body(i, _):
        cols = group(i)
        lam = spread(lam_ref, cols)
        step = jnp.exp(-ROWS * lam)
        acc = jnp.zeros_like(lam)
        gain = gain_ref[:, cols]
        gain_acc = jnp.zeros((16, LANES), F32)
        for a in range(length - 16, -1, -16):
            rows = slice(a, a + 16)
            inv = inv_ref[rows]
            q = q_ref[rows, cols].astype(F32)
            og = og_ref[rows, cols].astype(F32)
            conv = conv_ref[rows, cols]
            mixed = q * conv
            normed = mixed * inv
            y_ref[rows, cols] = (gain * normed).astype(BF16)
            gain_acc = gain_acc + og * normed
            mixed_grad = inv * (gain * og) - mixed * coef_ref[rows]
            gq_ref[rows, cols] = (mixed_grad * conv).astype(BF16)
            gate = mixed_grad * q
            gate_ref[rows, cols] = gate
            acc = acc * step + gate[None, ROWS:]
            acc = acc * step + gate[None, :ROWS]
        gain_part_ref[:, cols] = jnp.sum(gain_acc, axis=0, keepdims=True)
        weight = jnp.exp(-lam * (sublane() + 1.0))
        gw_ref[:, cols] = jnp.sum(acc * weight, axis=1)
        return 0

    lax.fori_loop(0, width // LANES, body, 0)


def backward_kernel(n_in, length_gap, *refs):
    pieces, slopes = refs[:n_in], refs[n_in : 2 * n_in]
    (lam_ref, res_ref, gate_ref, vs_ref, ks_ref, state_ref, gw_ref, gain_part_ref,
     fh_ref, fl_ref, th_ref, tl_ref, vg_ref, grads_ref, kg) = refs[2 * n_in :]
    length, width = gate_ref.shape
    gs = dot3(fh_ref[...], fl_ref[...], gate_ref[...])
    gr, gi = gs[:length], gs[length:]
    vr, vi = vs_ref[:length], vs_ref[length:]
    prod = jnp.concatenate([gr * vr + gi * vi, gi * vr - gr * vi], axis=0) * (1.0 / length)
    kg[...] = dot3(th_ref[...], tl_ref[...], prod)
    kr, ki = ks_ref[:length], ks_ref[length:]
    prod = jnp.concatenate([gr * kr + gi * ki, gi * kr - gr * ki], axis=0) * (1.0 / length)
    vg_ref[...] = dot3(th_ref[...], tl_ref[...], prod)

    def body(i, _):
        cols = group(i)
        lam = spread(lam_ref, cols)
        step = jnp.exp(-ROWS * lam)
        acc_r = jnp.zeros_like(lam)
        acc_s = jnp.zeros_like(lam)
        for a in range(length - ROWS, -1, -ROWS):
            tile = kg[a : a + ROWS, cols]
            acc_r = acc_r * step + tile[None]
            acc_s = acc_s * step + (tile * (sublane()[0] + float(a)))[None]
        weight = jnp.exp(-lam * sublane())
        part_r = jnp.sum(acc_r * weight, axis=1)
        part_s = jnp.sum(acc_s * weight, axis=1)
        acc_g = jnp.zeros_like(lam)
        for a in range(length - ROWS, -1, -ROWS):
            tile = gate_ref[a : a + ROWS, cols]
            acc_g = acc_g * step + (tile * (sublane()[0] + float(a + 1)))[None]
        g_one = jnp.sum(acc_g * jnp.exp(-lam * (sublane() + 1.0)), axis=1)
        lam_rows = lam_ref[:, cols]
        decay_block = jnp.exp(-length_gap * lam_rows)
        _, moved = combine([p[:, cols].astype(F32) for p in pieces], decay_block, length_gap)
        slope, _ = combine([p[:, cols].astype(F32) for p in slopes], decay_block, length_gap)
        state = state_ref[:, cols]
        gw = gw_ref[:, cols]
        total_r = part_r + gw * state
        total_s = part_s + g_one * state + gw * (slope + moved)
        modes = lam_rows.shape[0]
        grads_ref[i, :modes] = total_r.astype(grads_ref.dtype)
        grads_ref[i, modes : 2 * modes] = (-lam_rows * res_ref[:, cols] * total_s).astype(grads_ref.dtype)
        grads_ref[i, 2 * modes :] = jnp.broadcast_to(gain_part_ref[:, cols], (16, LANES)).astype(grads_ref.dtype)
        return 0

    lax.fori_loop(0, width // LANES, body, 0)


def finish_kernel(n_in, length_gap, *refs):
    pieces, (lam_ref, res_ref, vg_ref, k_ref, v_ref, gk_ref, gv_ref, held) = refs[:n_in], refs[n_in:]
    length, width = k_ref.shape

    def body(i, _):
        cols = group(i)
        decay_block = jnp.exp(-length_gap * lam_ref[:, cols])
        total, _ = combine([p[:, cols].astype(F32) for p in pieces], decay_block, length_gap)
        held[...] = total * res_ref[:, cols]
        lam = spread(lam_ref, cols)
        step = jnp.exp(-ROWS * lam)
        start = spread(held, slice(None)) * jnp.exp(-lam * (ROWS - 1 - sublane()))
        tiles = evaluate(start, step, length // ROWS)
        for a in range(length - 16, -1, -16):
            rows = slice(a, a + 16)
            upper = next(tiles)
            grad = vg_ref[rows, cols] + jnp.concatenate([next(tiles), upper], axis=0)
            gk_ref[rows, cols] = (grad * v_ref[rows, cols].astype(F32)).astype(BF16)
            gv_ref[rows, cols] = (grad * k_ref[rows, cols].astype(F32)).astype(BF16)
        return 0

    lax.fori_loop(0, width // LANES, body, 0)


def call(kernel, grid, ins, outs, scratch, flops):
    moved = sum(a.size * a.dtype.itemsize for a, _, _ in ins)
    moved += sum(int(np.prod(s)) * jnp.dtype(d).itemsize for s, d, _, _ in outs)
    return pl.pallas_call(
        kernel,
        grid=(grid,),
        in_specs=[pl.BlockSpec(b, m) for _, b, m in ins],
        out_specs=[pl.BlockSpec(b, m) for _, _, b, m in outs],
        out_shape=[jax.ShapeDtypeStruct(s, d) for s, d, _, _ in outs],
        scratch_shapes=scratch,
        compiler_params=pltpu.CompilerParams(
            dimension_semantics=("arbitrary",), vmem_limit_bytes=VMEM_LIMIT
        ),
        cost_estimate=pl.CostEstimate(flops=flops, bytes_accessed=moved, transcendentals=0),
    )(*[a for a, _, _ in ins])


def exchange(x, count, forward):
    if count <= 16:
        pieces = []
        for j in range(1, count):
            pairs = [(i, i + j) if forward else (i + j, i) for i in range(count - j)]
            pieces.append(lax.ppermute(x, "ctx", pairs))
        return pieces
    rank = lax.axis_index("ctx")
    every = lax.all_gather(x, "ctx")
    pieces = []
    for j in range(1, count):
        source = rank - j if forward else rank + j
        inside = (source >= 0) & (source < count)
        piece = lax.dynamic_index_in_dim(every, jnp.clip(source, 0, count - 1), 0, keepdims=False)
        pieces.append(jnp.where(inside, piece, jnp.zeros_like(piece)))
    return pieces


def shards(q_stream, k_stream, v_stream, out_grad, norm_gain, residue, rate):
    count = lax.axis_size("ctx")
    _, length, channels = q_stream.shape
    seq_len = length * count
    modes = residue.shape[1]
    model_width = float(channels * lax.axis_size("chan"))
    groups = channels // LANES
    width = min(channels, 512)
    grid = channels // width
    q, k, v, og = (x[0] for x in (q_stream, k_stream, v_stream, out_grad))
    lam = (jnp.exp(rate) / seq_len).T
    res = residue.T
    gain = norm_gain[None]
    full = fourier(length)
    fh, fl = halves(full)
    th, tl = halves(full.T)

    def wide(rows):
        return ((rows, width), lambda i: (0, i))

    def fixed(shape):
        return (shape, lambda i: (0,) * len(shape))

    def inputs(*arrays):
        return [(a, *wide(a.shape[0])) for a in arrays]

    def outputs(*rows_types):
        return [((r, channels), d, *wide(r)) for r, d in rows_types]

    basis = [(x, *fixed(x.shape)) for x in (fh, fl, th, tl)]
    unit = 2 * length * channels * modes

    vals, state = call(
        state_kernel, grid, inputs(k, v, lam), outputs((length, BF16), (modes, BF16)), [], unit
    )
    pieces = exchange(state, count, True)
    conv_local, vs, ks, slope = call(
        local_kernel, grid, inputs(vals, lam, res) + basis,
        outputs((length, F32), (2 * length, F32), (2 * length, F32), (modes, BF16)),
        [pltpu.VMEM((length, width), F32)], 16 * length * length * channels,
    )
    slopes = exchange(slope, count, True)
    sums_shape = (2, length, LANES)
    conv, sums, carried = call(
        functools.partial(forward_kernel, count - 1, float(length)), grid,
        inputs(*pieces, lam, res, conv_local, q, og, gain),
        outputs((length, F32)) + [(sums_shape, F32, *fixed(sums_shape))] + outputs((modes, F32)),
        [pltpu.VMEM((modes, LANES), F32)], unit,
    )
    peers = lax.ppermute(sums, "chan", [(0, 1), (1, 0)])
    y_out, grad_q, gate, gain_part, gw = call(
        functools.partial(gate_kernel, model_width), grid,
        [(sums, *fixed(sums_shape)), (peers, *fixed(sums_shape))] + inputs(lam, conv, q, og, gain),
        outputs((length, BF16), (length, BF16), (length, F32), (1, F32), (modes, F32)),
        [pltpu.VMEM((length, LANES), F32)] * 2, unit,
    )
    later = exchange(gw.astype(BF16), count, False)
    rows = 2 * modes + 16
    vg_local, grads = call(
        functools.partial(backward_kernel, count - 1, float(length)), grid,
        inputs(*pieces, *slopes, lam, res, gate, vs, ks, carried, gw, gain_part) + basis,
        outputs((length, F32))
        + [((groups, rows, LANES), BF16, (width // LANES, rows, LANES), lambda i: (i, 0, 0))],
        [pltpu.VMEM((length, width), F32)], 16 * length * length * channels,
    )
    grad_k, grad_v = call(
        functools.partial(finish_kernel, count - 1, float(length)), grid,
        inputs(*later, lam, res, vg_local, k, v),
        outputs((length, BF16), (length, BF16)),
        [pltpu.VMEM((modes, LANES), F32)], unit,
    )
    both = ("ctx", "dp")
    if count * lax.axis_size("dp") == groups:
        parts = lax.all_to_all(grads, both, 0, 0)
        mine = jnp.sum(parts.astype(F32), axis=0).astype(BF16)
        total = lax.all_to_all(jnp.broadcast_to(mine[None], grads.shape), both, 0, 0).astype(F32)
    else:
        total = lax.psum(grads.astype(F32), both)
    total = total.transpose(0, 2, 1).reshape(channels, rows)
    return (
        y_out[None],
        grad_q[None],
        grad_k[None],
        grad_v[None],
        total[:, :modes],
        total[:, modes : 2 * modes],
        total[:, 2 * modes],
    )


def solution(mesh):
    streams = P("dp", "ctx", "chan")
    in_specs = (streams,) * 4 + (P("chan"), P("chan", None), P("chan", None))
    out_specs = (streams,) * 4 + (P("chan", None), P("chan", None), P("chan"))
    return jax.shard_map(shards, mesh=mesh, in_specs=in_specs, out_specs=out_specs, check_vma=False)
```

```python
import functools

import jax
import jax.numpy as jnp
import numpy as np
from jax import lax
from jax.experimental import pallas as pl
from jax.experimental.pallas import tpu as pltpu
from jax.sharding import PartitionSpec as P

EPSILON = 1e-06
LANES = 128
ROWS = 8
F32 = jnp.float32
BF16 = jnp.bfloat16
VMEM_LIMIT = 20 * 1024 * 1024


def fourier(length):
    freq = 2 * np.arange(length)[:, None] + 1
    phase = (freq * np.arange(length)[None, :]) % (4 * length) * (2.0 * np.pi / (4 * length))
    full = np.concatenate([np.cos(phase), -np.sin(phase)], axis=0).astype(np.float32)
    return full


def halves(full):
    high = full.astype(jnp.bfloat16)
    low = (full - high.astype(np.float32)).astype(jnp.bfloat16)
    return jnp.asarray(high), jnp.asarray(low)


def split(x):
    high = x.astype(BF16)
    return high, (x - high.astype(F32)).astype(BF16)


def dot(a, b):
    return jnp.dot(a, b, preferred_element_type=F32)


def dot3(a_high, a_low, x):
    high, low = split(x)
    return dot(a_high, high) + (dot(a_high, low) + dot(a_low, high))


def spread(ref, cols):
    return jnp.stack(
        [jnp.broadcast_to(ref[m : m + 1, cols], (ROWS, LANES)) for m in range(ref.shape[0])]
    )


def sublane():
    return lax.broadcasted_iota(jnp.int32, (1, ROWS, LANES), 1).astype(F32)


def group(i):
    return pl.ds(pl.multiple_of(i * LANES, LANES), LANES)


def evaluate(start, step, tiles):
    term = start
    for i in range(tiles):
        yield jnp.sum(term, axis=0)
        if i + 1 < tiles:
            term = term * step


def gather_states(pieces_ref, cols, decay_block, forward):
    rank = lax.axis_index("ctx")
    count = pieces_ref.shape[0]
    total = jnp.zeros_like(decay_block)
    slope = jnp.zeros_like(decay_block)
    for s in range(count) if forward else range(count - 1, -1, -1):
        inside = (s < rank) if forward else (s > rank)
        piece = pieces_ref[s, :, cols].astype(F32)
        slope = jnp.where(inside, decay_block * (slope + total), slope)
        total = jnp.where(inside, decay_block * total + piece, total)
    return total, slope


def state_kernel(k_ref, v_ref, lam_ref, val_ref, s_ref):
    length, width = k_ref.shape

    def body(i, _):
        cols = group(i)
        lam = spread(lam_ref, cols)
        step = jnp.exp(-ROWS * lam)
        acc = jnp.zeros_like(lam)
        for a in range(0, length, 16):
            vals = (k_ref[a : a + 16, cols].astype(F32) * v_ref[a : a + 16, cols].astype(F32)).astype(BF16)
            val_ref[a : a + 16, cols] = vals
            vals = vals.astype(F32)
            acc = acc * step + vals[None, :ROWS]
            acc = acc * step + vals[None, ROWS:]
        weight = jnp.exp(-lam * (ROWS - 1 - sublane()))
        s_ref[:, cols] = jnp.sum(acc * weight, axis=1).astype(s_ref.dtype)
        return 0

    lax.fori_loop(0, width // LANES, body, 0)


def local_kernel(val_ref, lam_ref, res_ref, fh_ref, fl_ref, th_ref, tl_ref,
                 conv_ref, vs_ref, ks_ref, slope_ref, ker):
    length, width = val_ref.shape
    tiles = length // ROWS

    def body(i, _):
        cols = group(i)
        lam = spread(lam_ref, cols)
        step = jnp.exp(-ROWS * lam)
        start = spread(res_ref, cols) * jnp.exp(-lam * sublane())
        for a, tile in enumerate(evaluate(start, step, tiles)):
            ker[a * ROWS : (a + 1) * ROWS, cols] = tile
        acc = jnp.zeros_like(lam)
        for a in range(0, length, 16):
            vals = val_ref[a : a + 16, cols].astype(F32)
            for h in (0, ROWS):
                away = (length - 1 - a - h) - sublane()[0]
                acc = acc * step + (vals[h : h + ROWS] * away)[None]
        weight = jnp.exp(-lam * (ROWS - 1 - sublane()))
        slope_ref[:, cols] = jnp.sum(acc * weight, axis=1)
        return 0

    lax.fori_loop(0, width // LANES, body, 0)
    vals = val_ref[...]
    vs = dot(fh_ref[...], vals) + dot(fl_ref[...], vals)
    vs_ref[...] = vs
    ks = dot3(fh_ref[...], fl_ref[...], ker[...])
    ks_ref[...] = ks
    vr, vi = vs[:length], vs[length:]
    kr, ki = ks[:length], ks[length:]
    prod = jnp.concatenate([vr * kr - vi * ki, vr * ki + vi * kr], axis=0) * (1.0 / length)
    conv_ref[...] = dot3(th_ref[...], tl_ref[...], prod)


def forward_kernel(pieces_ref, lam_ref, res_ref, conv_in_ref, q_ref, og_ref, gain_ref,
                   conv_ref, sums_ref, state_ref, moved_ref, held):
    length, width = q_ref.shape

    @pl.when(pl.program_id(0) == 0)
    def _():
        sums_ref[...] = jnp.zeros_like(sums_ref)

    def body(i, _):
        cols = group(i)
        decay_block = jnp.exp(-float(length) * lam_ref[:, cols])
        total, moved = gather_states(pieces_ref, cols, decay_block, True)
        state_ref[:, cols] = total
        moved_ref[:, cols] = moved * float(length)
        held[...] = total * res_ref[:, cols]
        lam = spread(lam_ref, cols)
        step = jnp.exp(-ROWS * lam)
        start = spread(held, slice(None)) * jnp.exp(-lam * (sublane() + 1.0))
        gain = gain_ref[:, cols]
        tiles = evaluate(start, step, length // ROWS)
        for a in range(0, length, 16):
            rows = slice(a, a + 16)
            conv = conv_in_ref[rows, cols] + jnp.concatenate([next(tiles), next(tiles)], axis=0)
            conv_ref[rows, cols] = conv
            mixed = q_ref[rows, cols].astype(F32) * conv
            scaled = gain * og_ref[rows, cols].astype(F32)
            sums_ref[0, rows] += mixed * mixed
            sums_ref[1, rows] += scaled * mixed
        return 0

    lax.fori_loop(0, width // LANES, body, 0)


def gate_kernel(model_width, sums_ref, peer_ref, lam_ref, conv_ref, q_ref, og_ref, gain_ref,
                y_ref, gq_ref, gate_ref, gain_part_ref, gw_ref, inv_ref, coef_ref):
    length, width = q_ref.shape

    @pl.when(pl.program_id(0) == 0)
    def _():
        squares = jnp.sum(sums_ref[0] + peer_ref[0], axis=1, keepdims=True)
        inner = jnp.sum(sums_ref[1] + peer_ref[1], axis=1, keepdims=True)
        inv = lax.rsqrt(squares / model_width + EPSILON)
        coef = inv * inv * inv * inner / model_width
        inv_ref[...] = jnp.broadcast_to(inv, inv_ref.shape)
        coef_ref[...] = jnp.broadcast_to(coef, coef_ref.shape)

    def body(i, _):
        cols = group(i)
        lam = spread(lam_ref, cols)
        step = jnp.exp(-ROWS * lam)
        acc = jnp.zeros_like(lam)
        gain = gain_ref[:, cols]
        gain_acc = jnp.zeros((16, LANES), F32)
        for a in range(length - 16, -1, -16):
            rows = slice(a, a + 16)
            inv = inv_ref[rows]
            q = q_ref[rows, cols].astype(F32)
            og = og_ref[rows, cols].astype(F32)
            conv = conv_ref[rows, cols]
            mixed = q * conv
            normed = mixed * inv
            y_ref[rows, cols] = (gain * normed).astype(BF16)
            gain_acc = gain_acc + og * normed
            mixed_grad = inv * (gain * og) - mixed * coef_ref[rows]
            gq_ref[rows, cols] = (mixed_grad * conv).astype(BF16)
            gate = mixed_grad * q
            gate_ref[rows, cols] = gate
            acc = acc * step + gate[None, ROWS:]
            acc = acc * step + gate[None, :ROWS]
        gain_part_ref[:, cols] = jnp.sum(gain_acc, axis=0, keepdims=True)
        weight = jnp.exp(-lam * (sublane() + 1.0))
        gw_ref[:, cols] = jnp.sum(acc * weight, axis=1)
        return 0

    lax.fori_loop(0, width // LANES, body, 0)


def backward_kernel(lam_ref, res_ref, gate_ref, vs_ref, ks_ref, state_ref, moved_ref, gw_ref, gain_part_ref,
                    fh_ref, fl_ref, th_ref, tl_ref, vg_ref, grads_ref, kg):
    length, width = gate_ref.shape
    gs = dot3(fh_ref[...], fl_ref[...], gate_ref[...])
    gr, gi = gs[:length], gs[length:]
    vr, vi = vs_ref[:length], vs_ref[length:]
    prod = jnp.concatenate([gr * vr + gi * vi, gi * vr - gr * vi], axis=0) * (1.0 / length)
    kg[...] = dot3(th_ref[...], tl_ref[...], prod)
    kr, ki = ks_ref[:length], ks_ref[length:]
    prod = jnp.concatenate([gr * kr + gi * ki, gi * kr - gr * ki], axis=0) * (1.0 / length)
    vg_ref[...] = dot3(th_ref[...], tl_ref[...], prod)

    def body(i, _):
        cols = group(i)
        lam = spread(lam_ref, cols)
        step = jnp.exp(-ROWS * lam)
        acc_r = jnp.zeros_like(lam)
        acc_s = jnp.zeros_like(lam)
        for a in range(length - ROWS, -1, -ROWS):
            tile = kg[a : a + ROWS, cols]
            acc_r = acc_r * step + tile[None]
            acc_s = acc_s * step + (tile * (sublane()[0] + float(a)))[None]
        weight = jnp.exp(-lam * sublane())
        part_r = jnp.sum(acc_r * weight, axis=1)
        part_s = jnp.sum(acc_s * weight, axis=1)
        acc_g = jnp.zeros_like(lam)
        for a in range(length - ROWS, -1, -ROWS):
            tile = gate_ref[a : a + ROWS, cols]
            acc_g = acc_g * step + (tile * (sublane()[0] + float(a + 1)))[None]
        g_one = jnp.sum(acc_g * jnp.exp(-lam * (sublane() + 1.0)), axis=1)
        state = state_ref[:, cols]
        gw = gw_ref[:, cols]
        modes = gw.shape[0]
        grads_ref[i, :modes] = part_r + gw * state
        grads_ref[i, modes : 2 * modes] = part_s + g_one * state + gw * moved_ref[:, cols]
        grads_ref[i, 2 * modes :] = jnp.broadcast_to(gain_part_ref[:, cols], (16, LANES))
        return 0

    lax.fori_loop(0, width // LANES, body, 0)


def adjoint_kernel(length, pieces_ref, lam_ref, res_ref, slope_ref, grads_ref, adj_ref, out_ref):
    modes, width = lam_ref.shape

    def body(i, _):
        cols = group(i)
        lam = lam_ref[:, cols]
        total, _ = gather_states(pieces_ref, cols, jnp.exp(-length * lam), False)
        res = res_ref[:, cols]
        adj_ref[:, cols] = total * res
        out_ref[i, :modes] = grads_ref[i, :modes].astype(BF16)
        total_s = grads_ref[i, modes : 2 * modes] + slope_ref[:, cols] * total
        out_ref[i, modes : 2 * modes] = (-lam * res * total_s).astype(BF16)
        out_ref[i, 2 * modes :] = grads_ref[i, 2 * modes :].astype(BF16)
        return 0

    lax.fori_loop(0, width // LANES, body, 0)


def finish_kernel(adj_ref, lam_ref, vg_ref, k_ref, v_ref, gk_ref, gv_ref):
    length, width = k_ref.shape

    def body(i, _):
        cols = group(i)
        lam = spread(lam_ref, cols)
        step = jnp.exp(-ROWS * lam)
        start = spread(adj_ref, cols) * jnp.exp(-lam * (ROWS - 1 - sublane()))
        tiles = evaluate(start, step, length // ROWS)
        for a in range(length - 16, -1, -16):
            rows = slice(a, a + 16)
            upper = next(tiles)
            grad = vg_ref[rows, cols] + jnp.concatenate([next(tiles), upper], axis=0)
            gk_ref[rows, cols] = (grad * v_ref[rows, cols].astype(F32)).astype(BF16)
            gv_ref[rows, cols] = (grad * k_ref[rows, cols].astype(F32)).astype(BF16)
        return 0

    lax.fori_loop(0, width // LANES, body, 0)


def call(kernel, grid, ins, outs, scratch, flops):
    moved = sum(a.size * a.dtype.itemsize for a, _, _ in ins)
    moved += sum(int(np.prod(s)) * jnp.dtype(d).itemsize for s, d, _, _ in outs)
    return pl.pallas_call(
        kernel,
        grid=(grid,),
        in_specs=[pl.BlockSpec(b, m) for _, b, m in ins],
        out_specs=[pl.BlockSpec(b, m) for _, _, b, m in outs],
        out_shape=[jax.ShapeDtypeStruct(s, d) for s, d, _, _ in outs],
        scratch_shapes=scratch,
        compiler_params=pltpu.CompilerParams(
            dimension_semantics=("arbitrary",), vmem_limit_bytes=VMEM_LIMIT
        ),
        cost_estimate=pl.CostEstimate(flops=flops, bytes_accessed=moved, transcendentals=0),
    )(*[a for a, _, _ in ins])


def exchange(x, count):
    return lax.all_to_all(jnp.broadcast_to(x[None], (count,) + x.shape), "ctx", 0, 0)


def shards(q_stream, k_stream, v_stream, out_grad, norm_gain, residue, rate):
    count = lax.axis_size("ctx")
    _, length, channels = q_stream.shape
    seq_len = length * count
    modes = residue.shape[1]
    model_width = float(channels * lax.axis_size("chan"))
    groups = channels // LANES
    width = min(channels, 512)
    grid = channels // width
    q, k, v, og = (x[0] for x in (q_stream, k_stream, v_stream, out_grad))
    lam = (jnp.exp(rate) / seq_len).T
    res = residue.T
    gain = norm_gain[None]
    full = fourier(length)
    fh, fl = halves(full)
    th, tl = halves(full.T)

    def wide(rows):
        return ((rows, width), lambda i: (0, i))

    def fixed(shape):
        return (shape, lambda i: (0,) * len(shape))

    def inputs(*arrays):
        return [(a, *wide(a.shape[0])) for a in arrays]

    def outputs(*rows_types):
        return [((r, channels), d, *wide(r)) for r, d in rows_types]

    basis = [(x, *fixed(x.shape)) for x in (fh, fl, th, tl)]
    unit = 2 * length * channels * modes

    def stacked(array):
        return [(array, (array.shape[0], array.shape[1], width), lambda i: (0, 0, i))]

    k_far, v_far = (pltpu.with_memory_space_constraint(x, pltpu.HBM) for x in (k, v))
    vals, state = call(
        state_kernel, grid, inputs(k_far, v_far, lam), outputs((length, BF16), (modes, BF16)), [], unit
    )
    pieces = exchange(state, count)
    conv_local, vs, ks, slope = call(
        local_kernel, grid, inputs(vals, lam, res) + basis,
        outputs((length, F32), (2 * length, F32), (2 * length, F32), (modes, F32)),
        [pltpu.VMEM((length, width), F32)], 16 * length * length * channels,
    )
    sums_shape = (2, length, LANES)
    conv, sums, carried, moved = call(
        forward_kernel, grid,
        stacked(pieces) + inputs(lam, res, conv_local, q, og, gain),
        outputs((length, F32)) + [(sums_shape, F32, *fixed(sums_shape))] + outputs((modes, F32), (modes, F32)),
        [pltpu.VMEM((modes, LANES), F32)], unit,
    )
    peers = lax.ppermute(sums, "chan", [(0, 1), (1, 0)])
    y_out, grad_q, gate, gain_part, gw = call(
        functools.partial(gate_kernel, model_width), grid,
        [(sums, *fixed(sums_shape)), (peers, *fixed(sums_shape))] + inputs(lam, conv, q, og, gain),
        outputs((length, BF16), (length, BF16), (length, F32), (1, F32), (modes, F32)),
        [pltpu.VMEM((length, LANES), F32)] * 2, unit,
    )
    later = exchange(gw.astype(BF16), count)
    rows = 2 * modes + 16
    grads_shape = (groups, rows, LANES)
    grads_spec = ((width // LANES, rows, LANES), lambda i: (i, 0, 0))
    vg_local, grads = call(
        backward_kernel, grid,
        inputs(lam, res, gate, vs, ks, carried, moved, gw, gain_part) + basis,
        outputs((length, F32)) + [(grads_shape, F32, *grads_spec)],
        [pltpu.VMEM((length, width), F32)], 16 * length * length * channels,
    )
    adj, grads = call(
        functools.partial(adjoint_kernel, float(length)), grid,
        stacked(later) + inputs(lam, res, slope) + [(grads, *grads_spec)],
        outputs((modes, F32)) + [(grads_shape, BF16, *grads_spec)], [], channels * modes * 40,
    )
    grad_k, grad_v = call(
        finish_kernel, grid, inputs(adj, lam, vg_local, k, v),
        outputs((length, BF16), (length, BF16)), [], unit,
    )
    both = ("ctx", "dp")
    if count * lax.axis_size("dp") == groups:
        parts = lax.all_to_all(grads, both, 0, 0)
        mine = jnp.sum(parts.astype(F32), axis=0).astype(BF16)
        total = lax.all_to_all(jnp.broadcast_to(mine[None], grads.shape), both, 0, 0).astype(F32)
    else:
        total = lax.psum(grads.astype(F32), both)
    total = total.transpose(0, 2, 1).reshape(channels, rows)
    return (
        y_out[None],
        grad_q[None],
        grad_k[None],
        grad_v[None],
        total[:, :modes],
        total[:, modes : 2 * modes],
        total[:, 2 * modes],
    )


def solution(mesh):
    streams = P("dp", "ctx", "chan")
    in_specs = (streams,) * 4 + (P("chan"), P("chan", None), P("chan", None))
    out_specs = (streams,) * 4 + (P("chan", None), P("chan", None), P("chan"))
    return jax.shard_map(shards, mesh=mesh, in_specs=in_specs, out_specs=out_specs, check_vma=False)
```

```python
import functools

import jax
import jax.numpy as jnp
import numpy as np
from jax import lax
from jax.experimental import pallas as pl
from jax.experimental.pallas import tpu as pltpu
from jax.sharding import PartitionSpec as P

EPSILON = 1e-06
LANES = 128
ROWS = 8
F32 = jnp.float32
BF16 = jnp.bfloat16
VMEM_LIMIT = 20 * 1024 * 1024


def fourier(length):
    freq = 2 * np.arange(length)[:, None] + 1
    phase = (freq * np.arange(length)[None, :]) % (4 * length) * (2.0 * np.pi / (4 * length))
    full = np.concatenate([np.cos(phase), -np.sin(phase)], axis=0).astype(np.float32)
    return full


def halves(full):
    high = full.astype(jnp.bfloat16)
    low = (full - high.astype(np.float32)).astype(jnp.bfloat16)
    return jnp.asarray(high), jnp.asarray(low)


def split(x):
    high = x.astype(BF16)
    return high, (x - high.astype(F32)).astype(BF16)


def dot(a, b):
    return jnp.dot(a, b, preferred_element_type=F32)


def dot3(a_high, a_low, x):
    high, low = split(x)
    return dot(a_high, high) + (dot(a_high, low) + dot(a_low, high))


def spread(ref, cols):
    return jnp.stack(
        [jnp.broadcast_to(ref[m : m + 1, cols], (ROWS, LANES)) for m in range(ref.shape[0])]
    )


def sublane():
    return lax.broadcasted_iota(jnp.int32, (1, ROWS, LANES), 1).astype(F32)


def group(i):
    return pl.ds(pl.multiple_of(i * LANES, LANES), LANES)


def evaluate(start, step, tiles):
    term = start
    for i in range(tiles):
        yield jnp.sum(term, axis=0)
        if i + 1 < tiles:
            term = term * step


def gather_states(pieces_ref, cols, decay_block, forward):
    rank = lax.axis_index("ctx")
    count = pieces_ref.shape[0]
    total = jnp.zeros_like(decay_block)
    slope = jnp.zeros_like(decay_block)
    for s in range(count) if forward else range(count - 1, -1, -1):
        inside = (s < rank) if forward else (s > rank)
        piece = pieces_ref[s, :, cols].astype(F32)
        slope = jnp.where(inside, decay_block * (slope + total), slope)
        total = jnp.where(inside, decay_block * total + piece, total)
    return total, slope


def state_kernel(k_ref, v_ref, lam_ref, val_ref, s_ref):
    length, width = k_ref.shape

    def body(i, _):
        cols = group(i)
        lam = spread(lam_ref, cols)
        step = jnp.exp(-ROWS * lam)
        acc = jnp.zeros_like(lam)
        for a in range(0, length, 16):
            vals = (k_ref[a : a + 16, cols].astype(F32) * v_ref[a : a + 16, cols].astype(F32)).astype(BF16)
            val_ref[a : a + 16, cols] = vals
            vals = vals.astype(F32)
            acc = acc * step + vals[None, :ROWS]
            acc = acc * step + vals[None, ROWS:]
        weight = jnp.exp(-lam * (ROWS - 1 - sublane()))
        state = jnp.sum(acc * weight, axis=1).astype(BF16)
        for dest in range(s_ref.shape[0]):
            s_ref[dest, :, cols] = state
        return 0

    lax.fori_loop(0, width // LANES, body, 0)


def local_kernel(val_ref, lam_ref, res_ref, fh_ref, fl_ref, th_ref, tl_ref,
                 conv_ref, vs_ref, ks_ref, slope_ref, ker):
    length, width = val_ref.shape
    tiles = length // ROWS

    def body(i, _):
        cols = group(i)
        lam = spread(lam_ref, cols)
        step = jnp.exp(-ROWS * lam)
        start = spread(res_ref, cols) * jnp.exp(-lam * sublane())
        for a, tile in enumerate(evaluate(start, step, tiles)):
            ker[a * ROWS : (a + 1) * ROWS, cols] = tile
        acc = jnp.zeros_like(lam)
        for a in range(0, length, 16):
            vals = val_ref[a : a + 16, cols].astype(F32)
            for h in (0, ROWS):
                away = (length - 1 - a - h) - sublane()[0]
                acc = acc * step + (vals[h : h + ROWS] * away)[None]
        weight = jnp.exp(-lam * (ROWS - 1 - sublane()))
        slope_ref[:, cols] = jnp.sum(acc * weight, axis=1)
        return 0

    lax.fori_loop(0, width // LANES, body, 0)
    vals = val_ref[...]
    vs = dot(fh_ref[...], vals) + dot(fl_ref[...], vals)
    vs_ref[...] = vs
    ks = dot3(fh_ref[...], fl_ref[...], ker[...])
    ks_ref[...] = ks
    vr, vi = vs[:length], vs[length:]
    kr, ki = ks[:length], ks[length:]
    prod = jnp.concatenate([vr * kr - vi * ki, vr * ki + vi * kr], axis=0) * (1.0 / length)
    conv_ref[...] = dot3(th_ref[...], tl_ref[...], prod)


def forward_kernel(pieces_ref, lam_ref, res_ref, conv_in_ref, q_ref, og_ref, gain_ref,
                   conv_ref, sums_ref, state_ref, moved_ref, held):
    length, width = q_ref.shape

    @pl.when(pl.program_id(0) == 0)
    def _():
        sums_ref[...] = jnp.zeros_like(sums_ref)

    def body(i, _):
        cols = group(i)
        decay_block = jnp.exp(-float(length) * lam_ref[:, cols])
        total, moved = gather_states(pieces_ref, cols, decay_block, True)
        state_ref[:, cols] = total
        moved_ref[:, cols] = moved * float(length)
        held[...] = total * res_ref[:, cols]
        lam = spread(lam_ref, cols)
        step = jnp.exp(-ROWS * lam)
        start = spread(held, slice(None)) * jnp.exp(-lam * (sublane() + 1.0))
        gain = gain_ref[:, cols]
        tiles = evaluate(start, step, length // ROWS)
        for a in range(0, length, 16):
            rows = slice(a, a + 16)
            conv = conv_in_ref[rows, cols] + jnp.concatenate([next(tiles), next(tiles)], axis=0)
            conv_ref[rows, cols] = conv
            mixed = q_ref[rows, cols].astype(F32) * conv
            scaled = gain * og_ref[rows, cols].astype(F32)
            sums_ref[0, rows] += mixed * mixed
            sums_ref[1, rows] += scaled * mixed
        return 0

    lax.fori_loop(0, width // LANES, body, 0)


def gate_kernel(model_width, sums_ref, peer_ref, lam_ref, conv_ref, q_ref, og_ref, gain_ref,
                y_ref, gq_ref, gate_ref, gain_part_ref, gw_ref, send_ref, inv_ref, coef_ref):
    length, width = q_ref.shape

    @pl.when(pl.program_id(0) == 0)
    def _():
        squares = jnp.sum(sums_ref[0] + peer_ref[0], axis=1, keepdims=True)
        inner = jnp.sum(sums_ref[1] + peer_ref[1], axis=1, keepdims=True)
        inv = lax.rsqrt(squares / model_width + EPSILON)
        coef = inv * inv * inv * inner / model_width
        inv_ref[...] = jnp.broadcast_to(inv, inv_ref.shape)
        coef_ref[...] = jnp.broadcast_to(coef, coef_ref.shape)

    def body(i, _):
        cols = group(i)
        lam = spread(lam_ref, cols)
        step = jnp.exp(-ROWS * lam)
        acc = jnp.zeros_like(lam)
        gain = gain_ref[:, cols]
        gain_acc = jnp.zeros((16, LANES), F32)
        for a in range(length - 16, -1, -16):
            rows = slice(a, a + 16)
            inv = inv_ref[rows]
            q = q_ref[rows, cols].astype(F32)
            og = og_ref[rows, cols].astype(F32)
            conv = conv_ref[rows, cols]
            mixed = q * conv
            normed = mixed * inv
            y_ref[rows, cols] = (gain * normed).astype(BF16)
            gain_acc = gain_acc + og * normed
            mixed_grad = inv * (gain * og) - mixed * coef_ref[rows]
            gq_ref[rows, cols] = (mixed_grad * conv).astype(BF16)
            gate = mixed_grad * q
            gate_ref[rows, cols] = gate
            acc = acc * step + gate[None, ROWS:]
            acc = acc * step + gate[None, :ROWS]
        gain_part_ref[:, cols] = jnp.sum(gain_acc, axis=0, keepdims=True)
        weight = jnp.exp(-lam * (sublane() + 1.0))
        gw = jnp.sum(acc * weight, axis=1)
        gw_ref[:, cols] = gw
        for dest in range(send_ref.shape[0]):
            send_ref[dest, :, cols] = gw.astype(BF16)
        return 0

    lax.fori_loop(0, width // LANES, body, 0)


def backward_kernel(lam_ref, gate_ref, vs_ref, state_ref, moved_ref, gw_ref, gain_part_ref,
                    fh_ref, fl_ref, th_ref, tl_ref, gs_ref, grads_ref, kg):
    length, width = gate_ref.shape
    gs = dot3(fh_ref[...], fl_ref[...], gate_ref[...])
    gs_ref[...] = gs
    gr, gi = gs[:length], gs[length:]
    vr, vi = vs_ref[:length], vs_ref[length:]
    prod = jnp.concatenate([gr * vr + gi * vi, gi * vr - gr * vi], axis=0) * (1.0 / length)
    kg[...] = dot3(th_ref[...], tl_ref[...], prod)

    def body(i, _):
        cols = group(i)
        lam = spread(lam_ref, cols)
        step = jnp.exp(-ROWS * lam)
        acc_r = jnp.zeros_like(lam)
        acc_s = jnp.zeros_like(lam)
        for a in range(length - ROWS, -1, -ROWS):
            tile = kg[a : a + ROWS, cols]
            acc_r = acc_r * step + tile[None]
            acc_s = acc_s * step + (tile * (sublane()[0] + float(a)))[None]
        weight = jnp.exp(-lam * sublane())
        part_r = jnp.sum(acc_r * weight, axis=1)
        part_s = jnp.sum(acc_s * weight, axis=1)
        acc_g = jnp.zeros_like(lam)
        for a in range(length - ROWS, -1, -ROWS):
            tile = gate_ref[a : a + ROWS, cols]
            acc_g = acc_g * step + (tile * (sublane()[0] + float(a + 1)))[None]
        g_one = jnp.sum(acc_g * jnp.exp(-lam * (sublane() + 1.0)), axis=1)
        state = state_ref[:, cols]
        gw = gw_ref[:, cols]
        modes = gw.shape[0]
        grads_ref[i, :modes] = part_r + gw * state
        grads_ref[i, modes : 2 * modes] = part_s + g_one * state + gw * moved_ref[:, cols]
        grads_ref[i, 2 * modes :] = jnp.broadcast_to(gain_part_ref[:, cols], (16, LANES))
        return 0

    lax.fori_loop(0, width // LANES, body, 0)


def adjoint_kernel(length, pieces_ref, lam_ref, res_ref, slope_ref, grads_ref, adj_ref, out_ref):
    modes, width = lam_ref.shape

    def body(i, _):
        cols = group(i)
        lam = lam_ref[:, cols]
        total, _ = gather_states(pieces_ref, cols, jnp.exp(-length * lam), False)
        res = res_ref[:, cols]
        adj_ref[:, cols] = total * res
        out_ref[i, :modes] = grads_ref[i, :modes].astype(BF16)
        total_s = grads_ref[i, modes : 2 * modes] + slope_ref[:, cols] * total
        out_ref[i, modes : 2 * modes] = (-lam * res * total_s).astype(BF16)
        out_ref[i, 2 * modes :] = grads_ref[i, 2 * modes :].astype(BF16)
        return 0

    lax.fori_loop(0, width // LANES, body, 0)


def finish_kernel(adj_ref, lam_ref, gs_ref, ks_ref, k_ref, v_ref, th_ref, tl_ref, gk_ref, gv_ref, vg_ref):
    length, width = k_ref.shape
    gr, gi = gs_ref[:length], gs_ref[length:]
    kr, ki = ks_ref[:length], ks_ref[length:]
    prod = jnp.concatenate([gr * kr + gi * ki, gi * kr - gr * ki], axis=0) * (1.0 / length)
    vg_ref[...] = dot3(th_ref[...], tl_ref[...], prod)

    def body(i, _):
        cols = group(i)
        lam = spread(lam_ref, cols)
        step = jnp.exp(-ROWS * lam)
        start = spread(adj_ref, cols) * jnp.exp(-lam * (ROWS - 1 - sublane()))
        tiles = evaluate(start, step, length // ROWS)
        for a in range(length - 16, -1, -16):
            rows = slice(a, a + 16)
            upper = next(tiles)
            grad = vg_ref[rows, cols] + jnp.concatenate([next(tiles), upper], axis=0)
            gk_ref[rows, cols] = (grad * v_ref[rows, cols].astype(F32)).astype(BF16)
            gv_ref[rows, cols] = (grad * k_ref[rows, cols].astype(F32)).astype(BF16)
        return 0

    lax.fori_loop(0, width // LANES, body, 0)


def call(kernel, grid, ins, outs, scratch, flops):
    arrays = [e[0] if e[3:] else pltpu.with_memory_space_constraint(e[0], pltpu.HBM) for e in ins]
    moved = sum(a.size * a.dtype.itemsize for a in arrays)
    moved += sum(int(np.prod(s)) * jnp.dtype(d).itemsize for s, d, _, _ in outs)
    return pl.pallas_call(
        kernel,
        grid=(grid,),
        in_specs=[pl.BlockSpec(e[1], e[2]) for e in ins],
        out_specs=[pl.BlockSpec(b, m) for _, _, b, m in outs],
        out_shape=[pltpu.HBM(s, d) for s, d, _, _ in outs],
        scratch_shapes=scratch,
        compiler_params=pltpu.CompilerParams(
            dimension_semantics=("arbitrary",), vmem_limit_bytes=VMEM_LIMIT
        ),
        cost_estimate=pl.CostEstimate(flops=flops, bytes_accessed=moved, transcendentals=0),
    )(*arrays)


def shards(q_stream, k_stream, v_stream, out_grad, norm_gain, residue, rate):
    count = lax.axis_size("ctx")
    _, length, channels = q_stream.shape
    seq_len = length * count
    modes = residue.shape[1]
    model_width = float(channels * lax.axis_size("chan"))
    groups = channels // LANES
    width = min(channels, 512)
    grid = channels // width
    q, k, v, og = (x[0] for x in (q_stream, k_stream, v_stream, out_grad))
    lam = (jnp.exp(rate) / seq_len).T
    res = residue.T
    gain = norm_gain[None]
    full = fourier(length)
    fh, fl = halves(full)
    th, tl = halves(full.T)

    def wide(rows):
        return ((rows, width), lambda i: (0, i))

    def fixed(shape):
        return (shape, lambda i: (0,) * len(shape))

    def inputs(*arrays):
        return [(a, *wide(a.shape[0])) for a in arrays]

    def outputs(*rows_types):
        return [((r, channels), d, *wide(r)) for r, d in rows_types]

    basis = [(x, *fixed(x.shape)) for x in (fh, fl, th, tl)]
    unit = 2 * length * channels * modes

    def stacked(array):
        return [(array, (array.shape[0], array.shape[1], width), lambda i: (0, 0, i), True)]

    send_out = ((count, modes, channels), BF16, (count, modes, width), lambda i: (0, 0, i))
    vals, state = call(
        state_kernel, grid, inputs(k, v, lam), outputs((length, BF16)) + [send_out], [], unit
    )
    pieces = lax.all_to_all(state, "ctx", 0, 0)
    conv_local, vs, ks, slope = call(
        local_kernel, grid, inputs(vals, lam, res) + basis,
        outputs((length, F32), (2 * length, F32), (2 * length, F32), (modes, F32)),
        [pltpu.VMEM((length, width), F32)], 16 * length * length * channels,
    )
    sums_shape = (2, length, LANES)
    conv, sums, carried, moved = call(
        forward_kernel, grid,
        stacked(pieces) + inputs(lam, res, conv_local, q, og, gain),
        outputs((length, F32)) + [(sums_shape, F32, *fixed(sums_shape))] + outputs((modes, F32), (modes, F32)),
        [pltpu.VMEM((modes, LANES), F32)], unit,
    )
    peers = lax.ppermute(sums, "chan", [(0, 1), (1, 0)])
    y_out, grad_q, gate, gain_part, gw, send = call(
        functools.partial(gate_kernel, model_width), grid,
        [(sums, *fixed(sums_shape)), (peers, *fixed(sums_shape), True)] + inputs(lam, conv, q, og, gain),
        outputs((length, BF16), (length, BF16), (length, F32), (1, F32), (modes, F32)) + [send_out],
        [pltpu.VMEM((length, LANES), F32)] * 2, unit,
    )
    later = lax.all_to_all(send, "ctx", 0, 0)
    rows = 2 * modes + 16
    grads_shape = (groups, rows, LANES)
    grads_spec = ((width // LANES, rows, LANES), lambda i: (i, 0, 0))
    gs, grads = call(
        backward_kernel, grid,
        inputs(lam, gate, vs, carried, moved, gw, gain_part) + basis,
        outputs((2 * length, F32)) + [(grads_shape, F32, *grads_spec)],
        [pltpu.VMEM((length, width), F32)], 16 * length * length * channels,
    )
    adj, grads = call(
        functools.partial(adjoint_kernel, float(length)), grid,
        stacked(later) + inputs(lam, res, slope) + [(grads, *grads_spec)],
        outputs((modes, F32)) + [(grads_shape, BF16, *grads_spec)], [], channels * modes * 40,
    )
    grad_k, grad_v = call(
        finish_kernel, grid, inputs(adj, lam, gs, ks, k, v) + basis[2:],
        outputs((length, BF16), (length, BF16)), [pltpu.VMEM((length, width), F32)], unit,
    )
    both = ("ctx", "dp")
    if count * lax.axis_size("dp") == groups:
        parts = lax.all_to_all(grads, both, 0, 0)
        mine = jnp.sum(parts.astype(F32), axis=0).astype(BF16)
        total = lax.all_to_all(jnp.broadcast_to(mine[None], grads.shape), both, 0, 0).astype(F32)
    else:
        total = lax.psum(grads.astype(F32), both)
    total = total.transpose(0, 2, 1).reshape(channels, rows)
    return (
        y_out[None],
        grad_q[None],
        grad_k[None],
        grad_v[None],
        total[:, :modes],
        total[:, modes : 2 * modes],
        total[:, 2 * modes],
    )


def solution(mesh):
    streams = P("dp", "ctx", "chan")
    in_specs = (streams,) * 4 + (P("chan"), P("chan", None), P("chan", None))
    out_specs = (streams,) * 4 + (P("chan", None), P("chan", None), P("chan"))
    return jax.shard_map(shards, mesh=mesh, in_specs=in_specs, out_specs=out_specs, check_vma=False)
```

```python
import functools
import math

import jax
import jax.numpy as jnp
import numpy as np
from jax import lax
from jax.experimental import pallas as pl
from jax.experimental.pallas import tpu as pltpu
from jax.sharding import PartitionSpec as P

EPSILON = 1e-06
LANES = 128
ROWS = 8
F32 = jnp.float32
BF16 = jnp.bfloat16
MIB = 1024 * 1024


def fourier(length):
    freq = 2 * np.arange(length)[:, None] + 1
    phase = (freq * np.arange(length)[None, :]) % (4 * length) * (2.0 * np.pi / (4 * length))
    return np.concatenate([np.cos(phase), -np.sin(phase)], axis=0).astype(np.float32)


def terms(full, order):
    high = full.astype(jnp.bfloat16)
    low = (full - high.astype(np.float32)).astype(jnp.bfloat16)
    return jnp.asarray(np.concatenate([{"h": high, "l": low}[o] for o in order], axis=1))


def triple(x):
    high = x.astype(BF16)
    low = (x - high.astype(F32)).astype(BF16)
    return jnp.concatenate([high, low, high], axis=0)


def dot(a, b):
    return jnp.dot(a, b, preferred_element_type=F32)


def spread(ref, cols, first=0, count=16):
    return jnp.stack(
        [jnp.broadcast_to(ref[m : m + 1, cols], (ROWS, LANES)) for m in range(first, first + count)]
    )


def sublane():
    return lax.broadcasted_iota(jnp.int32, (ROWS, LANES), 0)


def fold(x):
    row = sublane()
    out = []
    for m in range(0, x.shape[0], ROWS):
        regs = [x[m + r] for r in range(ROWS)]
        for half in (4, 2, 1):
            low = (row & half) == 0
            regs = [
                jnp.where(
                    low,
                    regs[r] + pltpu.roll(regs[r], ROWS - half, 0),
                    regs[r + half] + pltpu.roll(regs[r + half], half, 0),
                )
                for r in range(half)
            ]
        out.append(regs[0])
    return jnp.concatenate(out, axis=0)


def groups_of(width, body):
    def step(i, _):
        body(i, pl.ds(pl.multiple_of(i * LANES, LANES), LANES))
        return 0

    lax.fori_loop(0, width // LANES, step, 0, unroll=UNROLL)


UNROLL = True


def evaluate(start, step, tiles):
    term = start
    for i in range(tiles):
        yield jnp.sum(term, axis=0)
        if i + 1 < tiles:
            term = term * step


def gather_states(pieces_ref, cols, decay_block, forward):
    rank = lax.axis_index("ctx")
    count = pieces_ref.shape[0]
    total = jnp.zeros_like(decay_block)
    slope = jnp.zeros_like(decay_block)
    for s in range(count) if forward else range(count - 1, -1, -1):
        inside = (s < rank) if forward else (s > rank)
        piece = pieces_ref[s, :, cols].astype(F32)
        if forward:
            slope = jnp.where(inside, decay_block * (slope + total), slope)
        total = jnp.where(inside, decay_block * total + piece, total)
    return total, slope


def state_kernel(seq_len, chunk, k_ref, v_ref, rate_ref, val_ref, lam_ref, parts_ref, send_ref):
    length, width = k_ref.shape

    def body(i, cols):
        lam_rows = jnp.exp(rate_ref[:, cols]) * (1.0 / seq_len)
        lam_ref[:, cols] = lam_rows
        lam = spread(lam_ref, cols)
        step = jnp.exp(-ROWS * lam)
        weight = jnp.exp(-lam * (ROWS - 1 - sublane()).astype(F32))
        decay_chunk = jnp.exp(-float(chunk) * lam_rows)
        total = None
        for c in range(length // chunk):
            acc = None
            for a in range(c * chunk, (c + 1) * chunk, 16):
                rows = slice(a, a + 16)
                vals = (k_ref[rows, cols].astype(F32) * v_ref[rows, cols].astype(F32)).astype(BF16)
                val_ref[rows, cols] = vals
                vals = vals.astype(F32)
                for tile in (vals[:ROWS], vals[ROWS:]):
                    acc = acc * step + tile[None] if acc is not None else jnp.broadcast_to(tile[None], lam.shape)
            part = fold(acc * weight)
            parts_ref[c, :, cols] = part
            total = part if total is None else total * decay_chunk + part
        for dest in range(send_ref.shape[0]):
            send_ref[dest, :, cols] = total.astype(BF16)

    groups_of(width, body)


def local_kernel(chunk, val_ref, lam_ref, res_ref, parts_ref, fv_ref, fa_ref, ta_ref,
                 conv_ref, ks_ref, slopes_ref, slope_ref, ker):
    length, width = val_ref.shape

    def body(i, cols):
        lam = spread(lam_ref, cols)
        step = jnp.exp(-ROWS * lam)
        row = sublane().astype(F32)
        start = spread(res_ref, cols) * jnp.exp(-lam * row)
        for a, tile in enumerate(evaluate(start, step, chunk // ROWS)):
            ker[a * ROWS : (a + 1) * ROWS, cols] = tile
        weight = jnp.exp(-lam * (ROWS - 1 - row))
        decay_chunk = jnp.exp(-float(chunk) * lam_ref[:, cols])
        total = slope = jnp.zeros_like(decay_chunk)
        for c in range(length // chunk):
            acc = None
            for a in range(0, chunk, 16):
                vals = val_ref[c * chunk + a : c * chunk + a + 16, cols].astype(F32)
                for h in (0, ROWS):
                    tile = (vals[h : h + ROWS] * (float(chunk - 1 - a - h) - row))[None]
                    acc = acc * step + tile if acc is not None else jnp.broadcast_to(tile, lam.shape)
            part = fold(acc * weight)
            slopes_ref[c, :, cols] = part
            slope = decay_chunk * (slope + float(chunk) * total) + part
            total = decay_chunk * total + parts_ref[c, :, cols]
        slope_ref[:, cols] = slope

    groups_of(width, body)
    ks = dot(fa_ref[...], triple(ker[...]))
    ks_ref[...] = ks
    kr, ki = ks[:chunk], ks[chunk:]
    for a in range(0, length, chunk):
        vals = val_ref[a : a + chunk]
        vs = dot(fv_ref[...], jnp.concatenate([vals, vals], axis=0))
        vr, vi = vs[:chunk], vs[chunk:]
        prod = jnp.concatenate([vr * kr - vi * ki, vr * ki + vi * kr], axis=0)
        conv_ref[a : a + chunk] = dot(ta_ref[...], triple(prod))


def forward_kernel(chunk, pieces_ref, lam_ref, res_ref, parts_ref, conv_in_ref, q_ref, og_ref, gain_ref,
                   conv_ref, sums_ref, states_ref, moved_ref, held):
    length, width = q_ref.shape

    @pl.when(pl.program_id(0) == 0)
    def _():
        sums_ref[...] = jnp.zeros_like(sums_ref)

    def body(i, cols):
        lam_rows = lam_ref[:, cols]
        modes = lam_rows.shape[0]
        state, moved = gather_states(pieces_ref, cols, jnp.exp(-float(length) * lam_rows), True)
        moved_ref[:, cols] = moved * float(length)
        decay_chunk = jnp.exp(-float(chunk) * lam_rows)
        res = res_ref[:, cols]
        for c in range(length // chunk):
            states_ref[c, :, cols] = state
            held[i, c * modes : (c + 1) * modes] = state * res
            state = decay_chunk * state + parts_ref[c, :, cols]
        lam = spread(lam_ref, cols)
        step = jnp.exp(-ROWS * lam)
        weight = jnp.exp(-lam * (sublane() + 1).astype(F32))
        gain = gain_ref[:, cols]
        for c in range(length // chunk):
            start = spread(held.at[i], slice(None), c * modes, modes) * weight
            tiles = evaluate(start, step, chunk // ROWS)
            for a in range(c * chunk, (c + 1) * chunk, 16):
                rows = slice(a, a + 16)
                conv = conv_in_ref[rows, cols] + jnp.concatenate([next(tiles), next(tiles)], axis=0)
                conv_ref[rows, cols] = conv
                mixed = q_ref[rows, cols].astype(F32) * conv
                scaled = gain * og_ref[rows, cols].astype(F32)
                sums_ref[0, rows] += mixed * mixed
                sums_ref[1, rows] += scaled * mixed

    groups_of(width, body)


def gate_kernel(model_width, chunk, sums_ref, peer_ref, lam_ref, conv_ref, q_ref, og_ref, gain_ref,
                y_ref, gq_ref, gate_ref, gain_part_ref, gw_ref, send_ref, inv_ref, coef_ref):
    length, width = q_ref.shape

    @pl.when(pl.program_id(0) == 0)
    def _():
        squares = jnp.sum(sums_ref[0] + peer_ref[0], axis=1, keepdims=True)
        inner = jnp.sum(sums_ref[1] + peer_ref[1], axis=1, keepdims=True)
        inv = lax.rsqrt(squares / model_width + EPSILON)
        coef = inv * inv * inv * inner / model_width
        inv_ref[...] = jnp.broadcast_to(inv, inv_ref.shape)
        coef_ref[...] = jnp.broadcast_to(coef, coef_ref.shape)

    def body(i, cols):
        lam = spread(lam_ref, cols)
        step = jnp.exp(-ROWS * lam)
        weight = jnp.exp(-lam * (sublane() + 1).astype(F32))
        decay_chunk = jnp.exp(-float(chunk) * lam_ref[:, cols])
        gain = gain_ref[:, cols]
        gain_acc = jnp.zeros((16, LANES), F32)
        total = None
        for c in range(length // chunk - 1, -1, -1):
            acc = None
            for a in range((c + 1) * chunk - 16, c * chunk - 1, -16):
                rows = slice(a, a + 16)
                inv = inv_ref[rows]
                q = q_ref[rows, cols].astype(F32)
                og = og_ref[rows, cols].astype(F32)
                conv = conv_ref[rows, cols]
                mixed = q * conv
                normed = mixed * inv
                y_ref[rows, cols] = (gain * normed).astype(BF16)
                gain_acc = gain_acc + og * normed
                mixed_grad = inv * (gain * og) - mixed * coef_ref[rows]
                gq_ref[rows, cols] = (mixed_grad * conv).astype(BF16)
                gate = mixed_grad * q
                gate_ref[rows, cols] = gate
                for tile in (gate[ROWS:], gate[:ROWS]):
                    acc = acc * step + tile[None] if acc is not None else jnp.broadcast_to(tile[None], lam.shape)
            part = fold(acc * weight)
            gw_ref[c, :, cols] = part
            total = part if total is None else total * decay_chunk + part
        gain_part_ref[:, cols] = jnp.sum(gain_acc, axis=0, keepdims=True)
        for dest in range(send_ref.shape[0]):
            send_ref[dest, :, cols] = total.astype(BF16)

    groups_of(width, body)


def backward_kernel(chunk, lam_ref, gate_ref, val_ref, ks_ref, states_ref, moved_ref, slopes_ref, gw_ref,
                    gain_part_ref, fv_ref, fa_ref, ta_ref, vg_ref, grads_ref, kg):
    length, width = gate_ref.shape
    kr, ki = ks_ref[:chunk], ks_ref[chunk:]
    cross_r = cross_i = None
    for a in range(0, length, chunk):
        gs = dot(fa_ref[...], triple(gate_ref[a : a + chunk]))
        gr, gi = gs[:chunk], gs[chunk:]
        vals = val_ref[a : a + chunk]
        vs = dot(fv_ref[...], jnp.concatenate([vals, vals], axis=0))
        vr, vi = vs[:chunk], vs[chunk:]
        real, imag = gr * vr + gi * vi, gi * vr - gr * vi
        cross_r = real if cross_r is None else cross_r + real
        cross_i = imag if cross_i is None else cross_i + imag
        prod = jnp.concatenate([gr * kr + gi * ki, gi * kr - gr * ki], axis=0)
        vg_ref[a : a + chunk] = dot(ta_ref[...], triple(prod))
    kg[...] = dot(ta_ref[...], triple(jnp.concatenate([cross_r, cross_i], axis=0)))

    def body(i, cols):
        lam_rows = lam_ref[:, cols]
        modes = lam_rows.shape[0]
        lam = spread(lam_ref, cols)
        row = sublane().astype(F32)
        step = jnp.exp(-ROWS * lam)
        acc_r = acc_s = jnp.zeros_like(lam)
        for a in range(chunk - ROWS, -1, -ROWS):
            tile = kg[a : a + ROWS, cols]
            acc_r = acc_r * step + tile[None]
            acc_s = acc_s * step + (tile * (row + float(a)))[None]
        weight = jnp.exp(-lam * row)
        total_r = fold(acc_r * weight)
        total_s = fold(acc_s * weight)
        weight = jnp.exp(-lam * (row + 1.0))
        decay_chunk = jnp.exp(-float(chunk) * lam_rows)
        slope = moved_ref[:, cols]
        for c in range(length // chunk):
            acc = None
            for a in range(chunk - ROWS, -1, -ROWS):
                tile = gate_ref[c * chunk + a : c * chunk + a + ROWS, cols] * (row + float(a + 1))
                acc = acc * step + tile[None] if acc is not None else jnp.broadcast_to(tile[None], lam.shape)
            g_one = fold(acc * weight)
            state = states_ref[c, :, cols]
            gw = gw_ref[c, :, cols]
            total_r = total_r + gw * state
            total_s = total_s + g_one * state + gw * slope
            slope = decay_chunk * (slope + float(chunk) * state) + slopes_ref[c, :, cols]
        grads_ref[i, :modes] = total_r
        grads_ref[i, modes : 2 * modes] = total_s
        grads_ref[i, 2 * modes :] = jnp.broadcast_to(gain_part_ref[:, cols], (16, LANES))

    groups_of(width, body)


def adjoint_kernel(length, pieces_ref, lam_ref, res_ref, slope_ref, grads_ref, adj_ref, out_ref):
    modes, width = lam_ref.shape

    def body(i, cols):
        lam = lam_ref[:, cols]
        total, _ = gather_states(pieces_ref, cols, jnp.exp(-length * lam), False)
        adj_ref[:, cols] = total
        out_ref[i, :modes] = grads_ref[i, :modes].astype(BF16)
        total_s = grads_ref[i, modes : 2 * modes] + slope_ref[:, cols] * total
        out_ref[i, modes : 2 * modes] = (-lam * res_ref[:, cols] * total_s).astype(BF16)
        out_ref[i, 2 * modes :] = grads_ref[i, 2 * modes :].astype(BF16)

    groups_of(width, body)


def finish_kernel(chunk, adj_ref, lam_ref, res_ref, gw_ref, vg_ref, k_ref, v_ref, gk_ref, gv_ref, held):
    length, width = k_ref.shape

    def body(i, cols):
        lam_rows = lam_ref[:, cols]
        modes = lam_rows.shape[0]
        decay_chunk = jnp.exp(-float(chunk) * lam_rows)
        adj = adj_ref[:, cols]
        res = res_ref[:, cols]
        for c in range(length // chunk - 1, -1, -1):
            held[i, c * modes : (c + 1) * modes] = adj * res
            adj = decay_chunk * adj + gw_ref[c, :, cols]
        lam = spread(lam_ref, cols)
        step = jnp.exp(-ROWS * lam)
        weight = jnp.exp(-lam * (ROWS - 1 - sublane()).astype(F32))
        for c in range(length // chunk - 1, -1, -1):
            start = spread(held.at[i], slice(None), c * modes, modes) * weight
            tiles = evaluate(start, step, chunk // ROWS)
            for a in range((c + 1) * chunk - 16, c * chunk - 1, -16):
                rows = slice(a, a + 16)
                upper = next(tiles)
                grad = vg_ref[rows, cols] + jnp.concatenate([next(tiles), upper], axis=0)
                gk_ref[rows, cols] = (grad * v_ref[rows, cols].astype(F32)).astype(BF16)
                gv_ref[rows, cols] = (grad * k_ref[rows, cols].astype(F32)).astype(BF16)

    groups_of(width, body)


def call(kernel, grid, ins, outs, scratch, flops, limit=16):
    arrays = [e[0] if e[3:] else pltpu.with_memory_space_constraint(e[0], pltpu.HBM) for e in ins]
    moved = sum(a.size * a.dtype.itemsize for a in arrays)
    moved += sum(int(np.prod(s)) * jnp.dtype(d).itemsize for s, d, _, _ in outs)
    return pl.pallas_call(
        kernel,
        grid=(grid,),
        in_specs=[pl.BlockSpec(e[1], e[2]) for e in ins],
        out_specs=[pl.BlockSpec(b, m) for _, _, b, m in outs],
        out_shape=[pltpu.HBM(s, d) for s, d, _, _ in outs],
        scratch_shapes=scratch,
        compiler_params=pltpu.CompilerParams(
            dimension_semantics=("arbitrary",), vmem_limit_bytes=limit * MIB
        ),
        cost_estimate=pl.CostEstimate(flops=flops, bytes_accessed=moved, transcendentals=0),
    )(*arrays)


def shards(q_stream, k_stream, v_stream, out_grad, norm_gain, residue, rate):
    count = lax.axis_size("ctx")
    _, length, channels = q_stream.shape
    seq_len = length * count
    modes = residue.shape[1]
    model_width = float(channels * lax.axis_size("chan"))
    chunk = math.gcd(length, 64)
    chunks = length // chunk
    groups = channels // LANES
    width = min(channels, 512)
    grid = channels // width
    q, k, v, og = (x[0] for x in (q_stream, k_stream, v_stream, out_grad))
    res = residue.T
    gain = norm_gain[None]
    full = fourier(chunk)
    basis = [terms(full, "hl"), terms(full, "hhl"), terms(full.T / np.float32(chunk), "hhl")]

    def block(shape, last=None):
        lead = tuple(shape[:-1])
        return (*lead, last or width), lambda i: (*(0 for _ in lead), i)

    def inputs(*arrays):
        return [(a, *block(a.shape)) for a in arrays]

    def outputs(*shapes_types):
        return [((*s, channels), d, *block((*s, channels))) for s, d in shapes_types]

    def fixed(shape):
        return shape, lambda i: (0,) * len(shape)

    basis = [(x, *fixed(x.shape)) for x in basis]
    unit = 2 * length * channels * modes
    send = ((count, modes), BF16)
    states = ((chunks, modes), F32)
    held = pltpu.VMEM((width // LANES, chunks * modes, LANES), F32)

    vals, lam, parts, state = call(
        functools.partial(state_kernel, float(seq_len), chunk), grid, inputs(k, v, rate.T),
        outputs(((length,), BF16), ((modes,), F32), states, send), [], unit,
    )
    pieces = lax.all_to_all(state, "ctx", 0, 0)
    conv_local, ks, slopes, slope = call(
        functools.partial(local_kernel, chunk), grid, inputs(vals, lam, res, parts) + basis,
        outputs(((length,), F32), ((2 * chunk,), F32), states, ((modes,), F32)),
        [pltpu.VMEM((chunk, width), F32)], 8 * unit,
    )
    sums_shape = (2, length, LANES)
    conv, sums, carried, moved = call(
        functools.partial(forward_kernel, chunk), grid,
        [(pieces, *block(pieces.shape), True)] + inputs(lam, res, parts, conv_local, q, og, gain),
        outputs(((length,), F32)) + [(sums_shape, F32, *fixed(sums_shape))] + outputs(states, ((modes,), F32)),
        [held], unit,
    )
    peers = lax.ppermute(sums, "chan", [(0, 1), (1, 0)])
    y_out, grad_q, gate, gain_part, gw, state = call(
        functools.partial(gate_kernel, model_width, chunk), grid,
        [(sums, *fixed(sums_shape)), (peers, *fixed(sums_shape), True)] + inputs(lam, conv, q, og, gain),
        outputs(((length,), BF16), ((length,), BF16), ((length,), F32), ((1,), F32), states, send),
        [pltpu.VMEM((length, LANES), F32)] * 2, unit,
    )
    later = lax.all_to_all(state, "ctx", 0, 0)
    rows = 2 * modes + 16
    grads_shape = (groups, rows, LANES)
    vg_local, grads = call(
        functools.partial(backward_kernel, chunk), grid,
        inputs(lam, gate, vals, ks, carried, moved, slopes, gw, gain_part) + basis,
        outputs(((length,), F32))
        + [(grads_shape, F32, (width // LANES, rows, LANES), lambda i: (i, 0, 0))],
        [pltpu.VMEM((chunk, width), F32)], 8 * unit,
    )
    adj, grads = call(
        functools.partial(adjoint_kernel, float(length)), 1,
        [(later, *fixed(later.shape), True)] + [(a, *fixed(a.shape)) for a in (lam, res, slope, grads)],
        [(lam.shape, F32, *fixed(lam.shape)), (grads_shape, BF16, *fixed(grads_shape))], [], channels * modes * 40,
    )
    grad_k, grad_v = call(
        functools.partial(finish_kernel, chunk), grid, inputs(adj, lam, res, gw, vg_local, k, v),
        outputs(((length,), BF16), ((length,), BF16)), [held], unit,
    )
    both = ("ctx", "dp")
    if count * lax.axis_size("dp") == groups:
        parts = lax.all_to_all(grads, both, 0, 0)
        mine = jnp.sum(parts.astype(F32), axis=0).astype(BF16)
        total = lax.all_to_all(jnp.broadcast_to(mine[None], grads.shape), both, 0, 0).astype(F32)
    else:
        total = lax.psum(grads.astype(F32), both)
    total = total.transpose(0, 2, 1).reshape(channels, rows)
    return (
        y_out[None],
        grad_q[None],
        grad_k[None],
        grad_v[None],
        total[:, :modes],
        total[:, modes : 2 * modes],
        total[:, 2 * modes],
    )


def solution(mesh):
    streams = P("dp", "ctx", "chan")
    in_specs = (streams,) * 4 + (P("chan"), P("chan", None), P("chan", None))
    out_specs = (streams,) * 4 + (P("chan", None), P("chan", None), P("chan"))
    return jax.shard_map(shards, mesh=mesh, in_specs=in_specs, out_specs=out_specs, check_vma=False)
```

```python
import functools
import math

import jax
import jax.numpy as jnp
import numpy as np
from jax import lax
from jax.experimental import pallas as pl
from jax.experimental.pallas import tpu as pltpu
from jax.sharding import PartitionSpec as P

EPSILON = 1e-06
LANES = 128
ROWS = 8
F32 = jnp.float32
BF16 = jnp.bfloat16
MIB = 1024 * 1024


def fourier(length):
    freq = 2 * np.arange(length)[:, None] + 1
    phase = (freq * np.arange(length)[None, :]) % (4 * length) * (2.0 * np.pi / (4 * length))
    return np.concatenate([np.cos(phase), -np.sin(phase)], axis=0).astype(np.float32)


def terms(full, order):
    high = full.astype(jnp.bfloat16)
    low = (full - high.astype(np.float32)).astype(jnp.bfloat16)
    return jnp.asarray(np.concatenate([{"h": high, "l": low}[o] for o in order], axis=1))


def triple(x):
    high = x.astype(BF16)
    low = (x - high.astype(F32)).astype(BF16)
    return jnp.concatenate([high, low, high], axis=0)


def dot(a, b):
    return jnp.dot(a, b, preferred_element_type=F32)


def spread(ref, cols, first=0, count=16):
    return jnp.stack(
        [jnp.broadcast_to(ref[m : m + 1, cols], (ROWS, LANES)) for m in range(first, first + count)]
    )


def sublane():
    return lax.broadcasted_iota(jnp.int32, (ROWS, LANES), 0)


def fold(x):
    row = sublane()
    out = []
    for m in range(0, x.shape[0], ROWS):
        regs = [x[m + r] for r in range(ROWS)]
        for half in (4, 2, 1):
            low = (row & half) == 0
            regs = [
                jnp.where(
                    low,
                    regs[r] + pltpu.roll(regs[r], ROWS - half, 0),
                    regs[r + half] + pltpu.roll(regs[r + half], half, 0),
                )
                for r in range(half)
            ]
        out.append(regs[0])
    return jnp.concatenate(out, axis=0)


def groups_of(width, body):
    def step(i, _):
        body(i, pl.ds(pl.multiple_of(i * LANES, LANES), LANES))
        return 0

    lax.fori_loop(0, width // LANES, step, 0, unroll=UNROLL)


UNROLL = True


def evaluate(start, step, tiles):
    term = start
    for i in range(tiles):
        yield jnp.sum(term, axis=0)
        if i + 1 < tiles:
            term = term * step


def gather_states(pieces_ref, cols, decay_block, forward):
    rank = lax.axis_index("ctx")
    count = pieces_ref.shape[0]
    total = jnp.zeros_like(decay_block)
    slope = jnp.zeros_like(decay_block)
    for s in range(count) if forward else range(count - 1, -1, -1):
        inside = (s < rank) if forward else (s > rank)
        piece = pieces_ref[s, :, cols].astype(F32)
        if forward:
            slope = jnp.where(inside, decay_block * (slope + total), slope)
        total = jnp.where(inside, decay_block * total + piece, total)
    return total, slope


def state_kernel(seq_len, chunk, k_ref, v_ref, rate_ref, val_ref, lam_ref, parts_ref, send_ref):
    length, width = k_ref.shape

    def body(i, cols):
        lam_rows = jnp.exp(rate_ref[:, cols]) * (1.0 / seq_len)
        lam_ref[:, cols] = lam_rows
        lam = spread(lam_ref, cols)
        step = jnp.exp(-ROWS * lam)
        weight = jnp.exp(-lam * (ROWS - 1 - sublane()).astype(F32))
        decay_chunk = jnp.exp(-float(chunk) * lam_rows)
        total = None
        for c in range(length // chunk):
            acc = None
            for a in range(c * chunk, (c + 1) * chunk, 16):
                rows = slice(a, a + 16)
                vals = (k_ref[rows, cols].astype(F32) * v_ref[rows, cols].astype(F32)).astype(BF16)
                val_ref[rows, cols] = vals
                vals = vals.astype(F32)
                for tile in (vals[:ROWS], vals[ROWS:]):
                    acc = acc * step + tile[None] if acc is not None else jnp.broadcast_to(tile[None], lam.shape)
            part = fold(acc * weight)
            parts_ref[c, :, cols] = part
            total = part if total is None else total * decay_chunk + part
        for dest in range(send_ref.shape[0]):
            send_ref[dest, :, cols] = total.astype(BF16)

    groups_of(width, body)


def local_kernel(chunk, val_ref, lam_ref, res_ref, parts_ref, fv_ref, fa_ref, ta_ref,
                 conv_ref, ks_ref, slopes_ref, slope_ref, ker):
    length, width = val_ref.shape

    def body(i, cols):
        lam = spread(lam_ref, cols)
        step = jnp.exp(-ROWS * lam)
        row = sublane().astype(F32)
        start = spread(res_ref, cols) * jnp.exp(-lam * row)
        for a, tile in enumerate(evaluate(start, step, chunk // ROWS)):
            ker[a * ROWS : (a + 1) * ROWS, cols] = tile
        weight = jnp.exp(-lam * (ROWS - 1 - row))
        decay_chunk = jnp.exp(-float(chunk) * lam_ref[:, cols])
        total = slope = jnp.zeros_like(decay_chunk)
        for c in range(length // chunk):
            acc = None
            for a in range(0, chunk, 16):
                vals = val_ref[c * chunk + a : c * chunk + a + 16, cols].astype(F32)
                for h in (0, ROWS):
                    tile = (vals[h : h + ROWS] * (float(chunk - 1 - a - h) - row))[None]
                    acc = acc * step + tile if acc is not None else jnp.broadcast_to(tile, lam.shape)
            part = fold(acc * weight)
            slopes_ref[c, :, cols] = part
            slope = decay_chunk * (slope + float(chunk) * total) + part
            total = decay_chunk * total + parts_ref[c, :, cols]
        slope_ref[:, cols] = slope

    groups_of(width, body)
    ks = dot(fa_ref[...], triple(ker[...]))
    ks_ref[...] = ks
    kr, ki = ks[:chunk], ks[chunk:]
    for a in range(0, length, chunk):
        vals = val_ref[a : a + chunk]
        vs = dot(fv_ref[...], jnp.concatenate([vals, vals], axis=0))
        vr, vi = vs[:chunk], vs[chunk:]
        prod = jnp.concatenate([vr * kr - vi * ki, vr * ki + vi * kr], axis=0)
        conv_ref[a : a + chunk] = dot(ta_ref[...], triple(prod))


def forward_begin(*refs):
    sums_ref = refs[9]
    sums_ref[...] = jnp.zeros_like(sums_ref)


def forward_kernel(chunk, lam_ref, res_ref, parts_ref, conv_in_ref, gain_ref, pieces_ref, q_ref, og_ref,
                   conv_ref, sums_ref, states_ref, moved_ref, held):
    length, width = q_ref.shape

    def body(i, cols):
        lam_rows = lam_ref[:, cols]
        modes = lam_rows.shape[0]
        state, moved = gather_states(pieces_ref, cols, jnp.exp(-float(length) * lam_rows), True)
        moved_ref[:, cols] = moved * float(length)
        decay_chunk = jnp.exp(-float(chunk) * lam_rows)
        res = res_ref[:, cols]
        for c in range(length // chunk):
            states_ref[c, :, cols] = state
            held[i, c * modes : (c + 1) * modes] = state * res
            state = decay_chunk * state + parts_ref[c, :, cols]
        lam = spread(lam_ref, cols)
        step = jnp.exp(-ROWS * lam)
        weight = jnp.exp(-lam * (sublane() + 1).astype(F32))
        gain = gain_ref[:, cols]
        for c in range(length // chunk):
            start = spread(held.at[i], slice(None), c * modes, modes) * weight
            tiles = evaluate(start, step, chunk // ROWS)
            for a in range(c * chunk, (c + 1) * chunk, 16):
                rows = slice(a, a + 16)
                conv = conv_in_ref[rows, cols] + jnp.concatenate([next(tiles), next(tiles)], axis=0)
                conv_ref[rows, cols] = conv
                mixed = q_ref[rows, cols].astype(F32) * conv
                scaled = gain * og_ref[rows, cols].astype(F32)
                sums_ref[0, rows] += mixed * mixed
                sums_ref[1, rows] += scaled * mixed

    groups_of(width, body)


def gate_begin(model_width, lam_ref, gain_ref, sums_ref, peer_ref, *refs):
    inv_ref, coef_ref = refs[-2:]
    squares = jnp.sum(sums_ref[0] + peer_ref[0], axis=1, keepdims=True)
    inner = jnp.sum(sums_ref[1] + peer_ref[1], axis=1, keepdims=True)
    inv = lax.rsqrt(squares / model_width + EPSILON)
    coef = inv * inv * inv * inner / model_width
    inv_ref[...] = jnp.broadcast_to(inv, inv_ref.shape)
    coef_ref[...] = jnp.broadcast_to(coef, coef_ref.shape)


def gate_kernel(chunk, lam_ref, gain_ref, sums_ref, peer_ref, conv_ref, q_ref, og_ref,
                y_ref, gq_ref, gate_ref, gain_part_ref, gw_ref, send_ref, inv_ref, coef_ref):
    length, width = q_ref.shape

    def body(i, cols):
        lam = spread(lam_ref, cols)
        step = jnp.exp(-ROWS * lam)
        weight = jnp.exp(-lam * (sublane() + 1).astype(F32))
        decay_chunk = jnp.exp(-float(chunk) * lam_ref[:, cols])
        gain = gain_ref[:, cols]
        gain_acc = jnp.zeros((16, LANES), F32)
        total = None
        for c in range(length // chunk - 1, -1, -1):
            acc = None
            for a in range((c + 1) * chunk - 16, c * chunk - 1, -16):
                rows = slice(a, a + 16)
                inv = inv_ref[rows]
                q = q_ref[rows, cols].astype(F32)
                og = og_ref[rows, cols].astype(F32)
                conv = conv_ref[rows, cols]
                mixed = q * conv
                normed = mixed * inv
                y_ref[rows, cols] = (gain * normed).astype(BF16)
                gain_acc = gain_acc + og * normed
                mixed_grad = inv * (gain * og) - mixed * coef_ref[rows]
                gq_ref[rows, cols] = (mixed_grad * conv).astype(BF16)
                gate = mixed_grad * q
                gate_ref[rows, cols] = gate
                for tile in (gate[ROWS:], gate[:ROWS]):
                    acc = acc * step + tile[None] if acc is not None else jnp.broadcast_to(tile[None], lam.shape)
            part = fold(acc * weight)
            gw_ref[c, :, cols] = part
            total = part if total is None else total * decay_chunk + part
        gain_part_ref[:, cols] = jnp.sum(gain_acc, axis=0, keepdims=True)
        for dest in range(send_ref.shape[0]):
            send_ref[dest, :, cols] = total.astype(BF16)

    groups_of(width, body)


def backward_kernel(chunk, lam_ref, gate_ref, val_ref, ks_ref, states_ref, moved_ref, slopes_ref, gw_ref,
                    gain_part_ref, fv_ref, fa_ref, ta_ref, vg_ref, grads_ref, kg):
    length, width = gate_ref.shape
    kr, ki = ks_ref[:chunk], ks_ref[chunk:]
    cross_r = cross_i = None
    for a in range(0, length, chunk):
        gs = dot(fa_ref[...], triple(gate_ref[a : a + chunk]))
        gr, gi = gs[:chunk], gs[chunk:]
        vals = val_ref[a : a + chunk]
        vs = dot(fv_ref[...], jnp.concatenate([vals, vals], axis=0))
        vr, vi = vs[:chunk], vs[chunk:]
        real, imag = gr * vr + gi * vi, gi * vr - gr * vi
        cross_r = real if cross_r is None else cross_r + real
        cross_i = imag if cross_i is None else cross_i + imag
        prod = jnp.concatenate([gr * kr + gi * ki, gi * kr - gr * ki], axis=0)
        vg_ref[a : a + chunk] = dot(ta_ref[...], triple(prod))
    kg[...] = dot(ta_ref[...], triple(jnp.concatenate([cross_r, cross_i], axis=0)))

    def body(i, cols):
        lam_rows = lam_ref[:, cols]
        modes = lam_rows.shape[0]
        lam = spread(lam_ref, cols)
        row = sublane().astype(F32)
        step = jnp.exp(-ROWS * lam)
        acc_r = acc_s = jnp.zeros_like(lam)
        for a in range(chunk - ROWS, -1, -ROWS):
            tile = kg[a : a + ROWS, cols]
            acc_r = acc_r * step + tile[None]
            acc_s = acc_s * step + (tile * (row + float(a)))[None]
        weight = jnp.exp(-lam * row)
        total_r = fold(acc_r * weight)
        total_s = fold(acc_s * weight)
        weight = jnp.exp(-lam * (row + 1.0))
        decay_chunk = jnp.exp(-float(chunk) * lam_rows)
        slope = moved_ref[:, cols]
        for c in range(length // chunk):
            acc = None
            for a in range(chunk - ROWS, -1, -ROWS):
                tile = gate_ref[c * chunk + a : c * chunk + a + ROWS, cols] * (row + float(a + 1))
                acc = acc * step + tile[None] if acc is not None else jnp.broadcast_to(tile[None], lam.shape)
            g_one = fold(acc * weight)
            state = states_ref[c, :, cols]
            gw = gw_ref[c, :, cols]
            total_r = total_r + gw * state
            total_s = total_s + g_one * state + gw * slope
            slope = decay_chunk * (slope + float(chunk) * state) + slopes_ref[c, :, cols]
        grads_ref[i, :modes] = total_r
        grads_ref[i, modes : 2 * modes] = total_s
        grads_ref[i, 2 * modes :] = jnp.broadcast_to(gain_part_ref[:, cols], (ROWS, LANES))

    groups_of(width, body)


def adjoint_kernel(length, lam_ref, res_ref, slope_ref, grads_ref, pieces_ref, adj_ref, out_ref):
    modes, width = lam_ref.shape

    def body(i, cols):
        lam = lam_ref[:, cols]
        total, _ = gather_states(pieces_ref, cols, jnp.exp(-length * lam), False)
        adj_ref[:, cols] = total
        out_ref[i, :modes] = grads_ref[i, :modes].astype(BF16)
        total_s = grads_ref[i, modes : 2 * modes] + slope_ref[:, cols] * total
        out_ref[i, modes : 2 * modes] = (-lam * res_ref[:, cols] * total_s).astype(BF16)
        out_ref[i, 2 * modes :] = grads_ref[i, 2 * modes :].astype(BF16)

    groups_of(width, body)


def finish_kernel(chunk, adj_ref, lam_ref, res_ref, gw_ref, vg_ref, k_ref, v_ref, gk_ref, gv_ref, held):
    length, width = k_ref.shape

    def body(i, cols):
        lam_rows = lam_ref[:, cols]
        modes = lam_rows.shape[0]
        decay_chunk = jnp.exp(-float(chunk) * lam_rows)
        adj = adj_ref[:, cols]
        res = res_ref[:, cols]
        for c in range(length // chunk - 1, -1, -1):
            held[i, c * modes : (c + 1) * modes] = adj * res
            adj = decay_chunk * adj + gw_ref[c, :, cols]
        lam = spread(lam_ref, cols)
        step = jnp.exp(-ROWS * lam)
        weight = jnp.exp(-lam * (ROWS - 1 - sublane()).astype(F32))
        for c in range(length // chunk - 1, -1, -1):
            start = spread(held.at[i], slice(None), c * modes, modes) * weight
            tiles = evaluate(start, step, chunk // ROWS)
            for a in range((c + 1) * chunk - 16, c * chunk - 1, -16):
                rows = slice(a, a + 16)
                upper = next(tiles)
                grad = vg_ref[rows, cols] + jnp.concatenate([next(tiles), upper], axis=0)
                gk_ref[rows, cols] = (grad * v_ref[rows, cols].astype(F32)).astype(BF16)
                gv_ref[rows, cols] = (grad * k_ref[rows, cols].astype(F32)).astype(BF16)

    groups_of(width, body)


def streamed(body, begin, steps, kinds_in, kinds_held, kinds_out, *refs):
    n_in, n_out = len(kinds_in), len(kinds_out)
    far_in, refs = refs[:n_in], refs[n_in:]
    here, refs = refs[: len(kinds_held)], refs[len(kinds_held) :]
    outs, refs = refs[:n_out], refs[n_out:]
    near_in, refs = refs[:n_in], refs[n_in:]
    away = [n for n, kind in enumerate(kinds_out) if not kind[2:]]
    far_out, kinds_far = [outs[n] for n in away], [kinds_out[n][1] for n in away]
    buffers, refs = refs[: len(away)], refs[len(away) :]
    near_out = list(outs)
    for n, buffer in zip(away, buffers):
        near_out[n] = buffer
    kinds_out = [kind[1] for kind in kinds_out]
    scratch, (sem_in, sem_out) = refs[:-2], refs[-2:]

    def view(ref, kind, b):
        if kind is None:
            return ref
        axis, size = kind
        start = b * size if axis == 0 else pl.multiple_of(b * size, LANES)
        return ref.at[(slice(None),) * axis + (pl.ds(start, size),)]

    def copies(far, near, kinds, sem, b, whole, outward):
        for n, kind in enumerate(kinds):
            if (kind is None) == whole:
                pair = view(far[n], kind, b), view(near[n], kind, b)
                source, target = pair[::-1] if outward else pair
                yield pltpu.make_async_copy(source, target, sem.at[b, n])

    for b in range(steps):
        for whole in (True, False) if b == 0 else (False,):
            for copy in copies(far_in, near_in, kinds_in, sem_in, b, whole, False):
                copy.start()
    for copy in copies(far_in, near_in, kinds_in, sem_in, 0, True, False):
        copy.wait()
    if begin is not None:
        begin(*near_in, *here, *near_out, *scratch)

    def step(b, _):
        for copy in copies(far_in, near_in, kinds_in, sem_in, b, False, False):
            copy.wait()
        body(
            *(view(r, k, b) for r, k in zip(near_in, kinds_in)),
            *(view(r, k, b) for r, k in zip(here, kinds_held)),
            *(view(r, k, b) for r, k in zip(near_out, kinds_out)),
            *scratch,
        )
        for copy in copies(far_out, buffers, kinds_far, sem_out, b, False, True):
            copy.start()
        return 0

    lax.fori_loop(0, steps, step, 0)
    for copy in copies(far_out, buffers, kinds_far, sem_out, 0, True, True):
        copy.start()
    for b in range(steps):
        for whole in (True, False) if b == 0 else (False,):
            for copy in copies(far_out, buffers, kinds_far, sem_out, b, whole, True):
                copy.wait()


def call(kernel, steps, ins, outs, scratch, flops, begin=None):
    here = [e for e in ins if e[2:]]
    ins = [e for e in ins if not e[2:]]
    arrays = [pltpu.with_memory_space_constraint(a, pltpu.HBM) for a, _ in ins]
    buffers = [(a.shape, a.dtype) for a in arrays] + [e[0] for e in outs if not e[2:]]
    moved = sum(int(np.prod(s)) * jnp.dtype(d).itemsize for s, d in buffers)
    far = pl.BlockSpec(memory_space=pltpu.HBM)
    near = pl.BlockSpec(memory_space=pltpu.VMEM)
    return pl.pallas_call(
        functools.partial(streamed, kernel, begin, steps, [k for _, k in ins], [e[1] for e in here], outs),
        in_specs=[far] * len(ins) + [near] * len(here),
        out_specs=[near if e[2:] else far for e in outs],
        out_shape=[jax.ShapeDtypeStruct(*e[0]) if e[2:] else pltpu.HBM(*e[0]) for e in outs],
        scratch_shapes=[pltpu.VMEM(s, d) for s, d in buffers]
        + scratch
        + [pltpu.SemaphoreType.DMA((steps, len(ins))), pltpu.SemaphoreType.DMA((steps, len(outs)))],
        compiler_params=pltpu.CompilerParams(vmem_limit_bytes=24 * MIB),
        cost_estimate=pl.CostEstimate(flops=flops, bytes_accessed=moved, transcendentals=0),
    )(*arrays, *(e[0] for e in here))


def shards(q_stream, k_stream, v_stream, out_grad, norm_gain, residue, rate):
    count = lax.axis_size("ctx")
    _, length, channels = q_stream.shape
    seq_len = length * count
    modes = residue.shape[1]
    model_width = float(channels * lax.axis_size("chan"))
    chunk = math.gcd(length, 64)
    chunks = length // chunk
    groups = channels // LANES
    width = min(channels, 512)
    grid = channels // width
    q, k, v, og = (x[0] for x in (q_stream, k_stream, v_stream, out_grad))
    res = residue.T
    gain = norm_gain[None]
    full = fourier(chunk)
    basis = [terms(full, "hl"), terms(full, "hhl"), terms(full.T / np.float32(chunk), "hhl")]
    basis = [(x, None) for x in basis]

    def inputs(*arrays):
        return [(a, (a.ndim - 1, width)) for a in arrays]

    def outputs(*shapes_types):
        return [(((*s, channels), d), (len(s), width)) for s, d in shapes_types]

    def held_inputs(*arrays):
        return [(a, (a.ndim - 1, width), True) for a in arrays]

    unit = 2 * length * channels * modes
    send = ((count, modes), BF16)
    states = ((chunks, modes), F32)
    held = pltpu.VMEM((width // LANES, chunks * modes, LANES), F32)

    vals, lam, parts, state = call(
        functools.partial(state_kernel, float(seq_len), chunk), grid, inputs(k, v, rate.T),
        outputs(((length,), BF16), ((modes,), F32), states, send), [], unit,
    )
    pieces = lax.all_to_all(state, "ctx", 0, 0)
    conv_local, ks, slopes, slope = call(
        functools.partial(local_kernel, chunk), grid, inputs(vals, lam, res, parts) + basis,
        outputs(((length,), F32), ((2 * chunk,), F32), states, ((modes,), F32)),
        [pltpu.VMEM((chunk, width), F32)], 8 * unit,
    )
    conv, sums, carried, moved = call(
        functools.partial(forward_kernel, chunk), grid,
        inputs(lam, res, parts, conv_local, gain) + held_inputs(pieces, q, og),
        [(((length, channels), F32), (1, width), True), (((2, length, LANES), F32), None, True)]
        + outputs(states, ((modes,), F32)),
        [held], unit, forward_begin,
    )
    peers = lax.ppermute(sums, "chan", [(0, 1), (1, 0)])
    y_out, grad_q, gate, gain_part, gw, state = call(
        functools.partial(gate_kernel, chunk), grid,
        inputs(lam, gain) + [(sums, None, True), (peers, None, True)] + held_inputs(conv, q, og),
        outputs(((length,), BF16), ((length,), BF16), ((length,), F32), ((1,), F32), states, send),
        [pltpu.VMEM((length, LANES), F32)] * 2, unit, functools.partial(gate_begin, model_width),
    )
    later = lax.all_to_all(state, "ctx", 0, 0)
    rows = 2 * modes + ROWS
    grads_shape = (groups, rows, LANES)
    vg_local, grads = call(
        functools.partial(backward_kernel, chunk), grid,
        inputs(lam, gate, vals, ks, carried, moved, slopes, gw, gain_part) + basis,
        outputs(((length,), F32)) + [((grads_shape, F32), (0, width // LANES))],
        [pltpu.VMEM((chunk, width), F32)], 8 * unit,
    )
    adj, grads = call(
        functools.partial(adjoint_kernel, float(length)), grid,
        inputs(lam, res, slope) + [(grads, (0, width // LANES)), (later, (2, width), True)],
        outputs(((modes,), F32)) + [((grads_shape, BF16), (0, width // LANES))], [], channels * modes * 40,
    )
    grad_k, grad_v = call(
        functools.partial(finish_kernel, chunk), grid, inputs(adj, lam, res, gw, vg_local) + held_inputs(k, v),
        outputs(((length,), BF16), ((length,), BF16)), [held], unit,
    )
    both = ("ctx", "dp")
    if count * lax.axis_size("dp") == groups:
        parts = lax.all_to_all(grads, both, 0, 0)
        mine = jnp.sum(parts.astype(F32), axis=0).astype(BF16)
        total = lax.all_to_all(jnp.broadcast_to(mine[None], grads.shape), both, 0, 0).astype(F32)
    else:
        total = lax.psum(grads.astype(F32), both)
    total = total.transpose(0, 2, 1).reshape(channels, rows)
    return (
        y_out[None],
        grad_q[None],
        grad_k[None],
        grad_v[None],
        total[:, :modes],
        total[:, modes : 2 * modes],
        total[:, 2 * modes],
    )


def solution(mesh):
    streams = P("dp", "ctx", "chan")
    in_specs = (streams,) * 4 + (P("chan"), P("chan", None), P("chan", None))
    out_specs = (streams,) * 4 + (P("chan", None), P("chan", None), P("chan"))
    return jax.shard_map(shards, mesh=mesh, in_specs=in_specs, out_specs=out_specs, check_vma=False)
```

```python
import functools
import math

import jax
import jax.numpy as jnp
import numpy as np
from jax import lax
from jax.experimental import pallas as pl
from jax.experimental.pallas import tpu as pltpu
from jax.sharding import PartitionSpec as P

EPSILON = 1e-06
LANES = 128
ROWS = 8
F32 = jnp.float32
BF16 = jnp.bfloat16
MIB = 1024 * 1024


def fourier(length):
    freq = 2 * np.arange(length)[:, None] + 1
    phase = (freq * np.arange(length)[None, :]) % (4 * length) * (2.0 * np.pi / (4 * length))
    return np.concatenate([np.cos(phase), -np.sin(phase)], axis=0).astype(np.float32)


def terms(full, order):
    high = full.astype(jnp.bfloat16)
    low = (full - high.astype(np.float32)).astype(jnp.bfloat16)
    pick = {"h": high, "l": low, "0": np.zeros_like(high)}
    return jnp.asarray(np.block([[pick[o] for o in row] for row in order]))


def triple(x):
    high = x.astype(BF16)
    low = (x - high.astype(F32)).astype(BF16)
    return jnp.concatenate([high, low, high], axis=0)


def inverse(t_ref, x):
    high = x.astype(BF16)
    low = (x - high.astype(F32)).astype(BF16)
    both = dot(t_ref[...], jnp.concatenate([high, low], axis=0))
    half = both.shape[0] // 2
    return both[:half] + both[half:]


def dot(a, b):
    return jnp.dot(a, b, preferred_element_type=F32)


def spread(ref, cols, first=0, count=16):
    return jnp.stack(
        [jnp.broadcast_to(ref[m : m + 1, cols], (ROWS, LANES)) for m in range(first, first + count)]
    )


def sublane():
    return lax.broadcasted_iota(jnp.int32, (ROWS, LANES), 0)


def fold(x):
    row = sublane()
    out = []
    for m in range(0, x.shape[0], ROWS):
        regs = [x[m + r] for r in range(ROWS)]
        for half in (4, 2, 1):
            low = (row & half) == 0
            regs = [
                jnp.where(
                    low,
                    regs[r] + pltpu.roll(regs[r], ROWS - half, 0),
                    regs[r + half] + pltpu.roll(regs[r + half], half, 0),
                )
                for r in range(half)
            ]
        out.append(regs[0])
    return jnp.concatenate(out, axis=0)


def groups_of(width, body):
    def step(i, _):
        body(i, pl.ds(pl.multiple_of(i * LANES, LANES), LANES))
        return 0

    lax.fori_loop(0, width // LANES, step, 0, unroll=UNROLL)


UNROLL = True


def evaluate(start, step, tiles):
    term = start
    for i in range(tiles):
        yield jnp.sum(term, axis=0)
        if i + 1 < tiles:
            term = term * step


def gather_states(pieces_ref, cols, decay_block, forward):
    rank = lax.axis_index("ctx")
    count = pieces_ref.shape[0]
    total = jnp.zeros_like(decay_block)
    slope = jnp.zeros_like(decay_block)
    for s in range(count) if forward else range(count - 1, -1, -1):
        inside = (s < rank) if forward else (s > rank)
        piece = pieces_ref[s, :, cols].astype(F32)
        if forward:
            slope = jnp.where(inside, decay_block * (slope + total), slope)
        total = jnp.where(inside, decay_block * total + piece, total)
    return total, slope


def state_kernel(seq_len, chunk, k_ref, v_ref, rate_ref, val_ref, lam_ref, parts_ref, send_ref):
    length, width = k_ref.shape

    def body(i, cols):
        lam_rows = jnp.exp(rate_ref[:, cols]) * (1.0 / seq_len)
        lam_ref[:, cols] = lam_rows
        lam = spread(lam_ref, cols)
        step = jnp.exp(-ROWS * lam)
        weight = jnp.exp(-lam * (ROWS - 1 - sublane()).astype(F32))
        decay_chunk = jnp.exp(-float(chunk) * lam_rows)
        total = None
        for c in range(length // chunk):
            acc = None
            for a in range(c * chunk, (c + 1) * chunk, 16):
                rows = slice(a, a + 16)
                vals = k_ref[rows, cols] * v_ref[rows, cols]
                val_ref[rows, cols] = vals
                vals = vals.astype(F32)
                for tile in (vals[:ROWS], vals[ROWS:]):
                    acc = acc * step + tile[None] if acc is not None else jnp.broadcast_to(tile[None], lam.shape)
            part = fold(acc * weight)
            parts_ref[c, :, cols] = part
            total = part if total is None else total * decay_chunk + part
        for dest in range(send_ref.shape[0]):
            send_ref[dest, :, cols] = total.astype(BF16)

    groups_of(width, body)


def local_kernel(chunk, val_ref, lam_ref, res_ref, parts_ref, fv_ref, fa_ref, ta_ref,
                 conv_ref, ks_ref, slopes_ref, slope_ref, ker):
    length, width = val_ref.shape

    def body(i, cols):
        lam = spread(lam_ref, cols)
        step = jnp.exp(-ROWS * lam)
        row = sublane().astype(F32)
        start = spread(res_ref, cols) * jnp.exp(-lam * row)
        for a, tile in enumerate(evaluate(start, step, chunk // ROWS)):
            ker[a * ROWS : (a + 1) * ROWS, cols] = tile
        weight = jnp.exp(-lam * (ROWS - 1 - row))
        decay_chunk = jnp.exp(-float(chunk) * lam_ref[:, cols])
        total = slope = jnp.zeros_like(decay_chunk)
        for c in range(length // chunk):
            acc = None
            for a in range(0, chunk, 16):
                vals = val_ref[c * chunk + a : c * chunk + a + 16, cols].astype(F32)
                for h in (0, ROWS):
                    tile = (vals[h : h + ROWS] * (float(chunk - 1 - a - h) - row))[None]
                    acc = acc * step + tile if acc is not None else jnp.broadcast_to(tile, lam.shape)
            part = fold(acc * weight)
            slopes_ref[c, :, cols] = part
            slope = decay_chunk * (slope + float(chunk) * total) + part
            total = decay_chunk * total + parts_ref[c, :, cols]
        slope_ref[:, cols] = slope

    groups_of(width, body)
    ks = dot(fa_ref[...], triple(ker[...]))
    ks_ref[...] = ks
    kr, ki = ks[:chunk], ks[chunk:]
    for a in range(0, length, chunk):
        vals = val_ref[a : a + chunk]
        vs = dot(fv_ref[...], jnp.concatenate([vals, vals], axis=0))
        vr, vi = vs[:chunk], vs[chunk:]
        prod = jnp.concatenate([vr * kr - vi * ki, vr * ki + vi * kr], axis=0)
        conv_ref[a : a + chunk] = inverse(ta_ref, prod)


def forward_begin(*refs):
    acc_ref = refs[-1]
    acc_ref[...] = jnp.zeros_like(acc_ref)


def forward_end(*refs):
    sums_ref, acc_ref = refs[9], refs[-1]
    for n in range(2):
        sums_ref[n : n + 1] = jnp.sum(acc_ref[n].T, axis=0, keepdims=True)


def forward_kernel(chunk, lam_ref, res_ref, parts_ref, conv_in_ref, gain_ref, pieces_ref, q_ref, og_ref,
                   conv_ref, sums_ref, states_ref, moved_ref, held, acc_ref):
    length, width = q_ref.shape

    def body(i, cols):
        lam_rows = lam_ref[:, cols]
        modes = lam_rows.shape[0]
        state, moved = gather_states(pieces_ref, cols, jnp.exp(-float(length) * lam_rows), True)
        moved_ref[:, cols] = moved * float(length)
        decay_chunk = jnp.exp(-float(chunk) * lam_rows)
        res = res_ref[:, cols]
        for c in range(length // chunk):
            states_ref[c, :, cols] = state
            held[i, c * modes : (c + 1) * modes] = state * res
            state = decay_chunk * state + parts_ref[c, :, cols]
        lam = spread(lam_ref, cols)
        step = jnp.exp(-ROWS * lam)
        weight = jnp.exp(-lam * (sublane() + 1).astype(F32))
        gain = gain_ref[:, cols]
        for c in range(length // chunk):
            start = spread(held.at[i], slice(None), c * modes, modes) * weight
            tiles = evaluate(start, step, chunk // ROWS)
            for a in range(c * chunk, (c + 1) * chunk, 16):
                rows = slice(a, a + 16)
                conv = conv_in_ref[rows, cols] + jnp.concatenate([next(tiles), next(tiles)], axis=0)
                conv_ref[rows, cols] = conv
                mixed = q_ref[rows, cols].astype(F32) * conv
                scaled = gain * og_ref[rows, cols].astype(F32)
                acc_ref[0, rows] += mixed * mixed
                acc_ref[1, rows] += scaled * mixed

    groups_of(width, body)


def gate_begin(model_width, lam_ref, gain_ref, sums_ref, peer_ref, *refs):
    inv_ref, coef_ref = refs[-2:]
    squares = sums_ref[0:1] + peer_ref[0:1]
    inner = sums_ref[1:2] + peer_ref[1:2]
    inv = lax.rsqrt(squares / model_width + EPSILON)
    coef = inv * inv * inv * inner / model_width
    for row, ref in ((inv, inv_ref), (coef, coef_ref)):
        ref[...] = jnp.broadcast_to(row, (LANES, row.shape[1])).T


def gate_kernel(chunk, lam_ref, gain_ref, sums_ref, peer_ref, conv_ref, q_ref, og_ref,
                y_ref, gq_ref, gate_ref, gain_part_ref, gw_ref, send_ref, inv_ref, coef_ref):
    length, width = q_ref.shape

    def body(i, cols):
        lam = spread(lam_ref, cols)
        step = jnp.exp(-ROWS * lam)
        weight = jnp.exp(-lam * (sublane() + 1).astype(F32))
        decay_chunk = jnp.exp(-float(chunk) * lam_ref[:, cols])
        gain = gain_ref[:, cols]
        gain_acc = jnp.zeros((16, LANES), F32)
        total = None
        for c in range(length // chunk - 1, -1, -1):
            acc = None
            for a in range((c + 1) * chunk - 16, c * chunk - 1, -16):
                rows = slice(a, a + 16)
                inv = inv_ref[rows]
                q = q_ref[rows, cols].astype(F32)
                og = og_ref[rows, cols].astype(F32)
                conv = conv_ref[rows, cols]
                mixed = q * conv
                normed = mixed * inv
                y_ref[rows, cols] = (gain * normed).astype(BF16)
                gain_acc = gain_acc + og * normed
                mixed_grad = inv * (gain * og) - mixed * coef_ref[rows]
                gq_ref[rows, cols] = (mixed_grad * conv).astype(BF16)
                gate = mixed_grad * q
                gate_ref[rows, cols] = gate
                for tile in (gate[ROWS:], gate[:ROWS]):
                    acc = acc * step + tile[None] if acc is not None else jnp.broadcast_to(tile[None], lam.shape)
            part = fold(acc * weight)
            gw_ref[c, :, cols] = part
            total = part if total is None else total * decay_chunk + part
        gain_part_ref[:, cols] = jnp.sum(gain_acc, axis=0, keepdims=True)
        for dest in range(send_ref.shape[0]):
            send_ref[dest, :, cols] = total.astype(BF16)

    groups_of(width, body)


def backward_kernel(chunk, lam_ref, gate_ref, val_ref, ks_ref, states_ref, moved_ref, slopes_ref, gw_ref,
                    gain_part_ref, fv_ref, fa_ref, ta_ref, vg_ref, grads_ref, kg):
    length, width = gate_ref.shape
    kr, ki = ks_ref[:chunk], ks_ref[chunk:]
    cross_r = cross_i = None
    for a in range(0, length, chunk):
        gs = dot(fa_ref[...], triple(gate_ref[a : a + chunk]))
        gr, gi = gs[:chunk], gs[chunk:]
        vals = val_ref[a : a + chunk]
        vs = dot(fv_ref[...], jnp.concatenate([vals, vals], axis=0))
        vr, vi = vs[:chunk], vs[chunk:]
        real, imag = gr * vr + gi * vi, gi * vr - gr * vi
        cross_r = real if cross_r is None else cross_r + real
        cross_i = imag if cross_i is None else cross_i + imag
        prod = jnp.concatenate([gr * kr + gi * ki, gi * kr - gr * ki], axis=0)
        vg_ref[a : a + chunk] = inverse(ta_ref, prod)
    kg[...] = inverse(ta_ref, jnp.concatenate([cross_r, cross_i], axis=0))

    def body(i, cols):
        lam_rows = lam_ref[:, cols]
        modes = lam_rows.shape[0]
        lam = spread(lam_ref, cols)
        row = sublane().astype(F32)
        step = jnp.exp(-ROWS * lam)
        acc_r = acc_s = jnp.zeros_like(lam)
        for a in range(chunk - ROWS, -1, -ROWS):
            tile = kg[a : a + ROWS, cols]
            acc_r = acc_r * step + tile[None]
            acc_s = acc_s * step + (tile * (row + float(a)))[None]
        weight = jnp.exp(-lam * row)
        total_r = fold(acc_r * weight)
        total_s = fold(acc_s * weight)
        weight = jnp.exp(-lam * (row + 1.0))
        decay_chunk = jnp.exp(-float(chunk) * lam_rows)
        slope = moved_ref[:, cols]
        for c in range(length // chunk):
            acc = None
            for a in range(chunk - ROWS, -1, -ROWS):
                tile = gate_ref[c * chunk + a : c * chunk + a + ROWS, cols] * (row + float(a + 1))
                acc = acc * step + tile[None] if acc is not None else jnp.broadcast_to(tile[None], lam.shape)
            g_one = fold(acc * weight)
            state = states_ref[c, :, cols]
            gw = gw_ref[c, :, cols]
            total_r = total_r + gw * state
            total_s = total_s + g_one * state + gw * slope
            slope = decay_chunk * (slope + float(chunk) * state) + slopes_ref[c, :, cols]
        grads_ref[i, :modes] = total_r
        grads_ref[i, modes : 2 * modes] = total_s
        grads_ref[i, 2 * modes :] = jnp.broadcast_to(gain_part_ref[:, cols], (ROWS, LANES))

    groups_of(width, body)


def adjoint_kernel(length, grads_ref, lam_ref, res_ref, slope_ref, pieces_ref, adj_ref, out_ref):
    modes, width = lam_ref.shape

    def body(i, cols):
        lam = lam_ref[:, cols]
        total, _ = gather_states(pieces_ref, cols, jnp.exp(-length * lam), False)
        adj_ref[:, cols] = total
        out_ref[i, :modes] = grads_ref[i, :modes].astype(BF16)
        total_s = grads_ref[i, modes : 2 * modes] + slope_ref[:, cols] * total
        out_ref[i, modes : 2 * modes] = (-lam * res_ref[:, cols] * total_s).astype(BF16)
        out_ref[i, 2 * modes :] = grads_ref[i, 2 * modes :].astype(BF16)

    groups_of(width, body)


def finish_kernel(chunk, adj_ref, lam_ref, res_ref, gw_ref, vg_ref, k_ref, v_ref, gk_ref, gv_ref, held):
    length, width = k_ref.shape

    def body(i, cols):
        lam_rows = lam_ref[:, cols]
        modes = lam_rows.shape[0]
        decay_chunk = jnp.exp(-float(chunk) * lam_rows)
        adj = adj_ref[:, cols]
        res = res_ref[:, cols]
        for c in range(length // chunk - 1, -1, -1):
            held[i, c * modes : (c + 1) * modes] = adj * res
            adj = decay_chunk * adj + gw_ref[c, :, cols]
        lam = spread(lam_ref, cols)
        step = jnp.exp(-ROWS * lam)
        weight = jnp.exp(-lam * (ROWS - 1 - sublane()).astype(F32))
        for c in range(length // chunk - 1, -1, -1):
            start = spread(held.at[i], slice(None), c * modes, modes) * weight
            tiles = evaluate(start, step, chunk // ROWS)
            for a in range((c + 1) * chunk - 16, c * chunk - 1, -16):
                rows = slice(a, a + 16)
                upper = next(tiles)
                grad = vg_ref[rows, cols] + jnp.concatenate([next(tiles), upper], axis=0)
                gk_ref[rows, cols] = (grad * v_ref[rows, cols].astype(F32)).astype(BF16)
                gv_ref[rows, cols] = (grad * k_ref[rows, cols].astype(F32)).astype(BF16)

    groups_of(width, body)


def streamed(body, begin, end, steps, kinds_in, kinds_out, *refs):
    ins, refs = refs[: len(kinds_in)], refs[len(kinds_in) :]
    outs, refs = refs[: len(kinds_out)], refs[len(kinds_out) :]

    def buffered(arrays, kinds, refs):
        away = [n for n, kind in enumerate(kinds) if not kind[2:]]
        near = list(arrays)
        for n, buffer in zip(away, refs):
            near[n] = buffer
        far = [arrays[n] for n in away]
        return near, far, refs[: len(away)], [kinds[n][1] for n in away], refs[len(away) :]

    near_in, far_in, buffers_in, moved_in, refs = buffered(ins, kinds_in, refs)
    near_out, far_out, buffers_out, moved_out, refs = buffered(outs, kinds_out, refs)
    kinds_in, kinds_out = [kind[1] for kind in kinds_in], [kind[1] for kind in kinds_out]
    scratch, (sem_in, sem_out) = refs[:-2], refs[-2:]

    def view(ref, kind, b):
        if kind is None:
            return ref
        axis, size = kind
        start = b * size if axis == 0 else pl.multiple_of(b * size, LANES)
        return ref.at[(slice(None),) * axis + (pl.ds(start, size),)]

    def copies(far, near, kinds, sem, b, whole, outward):
        for n, kind in enumerate(kinds):
            if (kind is None) == whole:
                pair = view(far[n], kind, b), view(near[n], kind, b)
                source, target = pair[::-1] if outward else pair
                yield pltpu.make_async_copy(source, target, sem.at[b, n])

    for b in range(steps):
        for whole in (True, False) if b == 0 else (False,):
            for copy in copies(far_in, buffers_in, moved_in, sem_in, b, whole, False):
                copy.start()
    for copy in copies(far_in, buffers_in, moved_in, sem_in, 0, True, False):
        copy.wait()
    if begin is not None:
        begin(*near_in, *near_out, *scratch)

    def step(b, _):
        for copy in copies(far_in, buffers_in, moved_in, sem_in, b, False, False):
            copy.wait()
        body(
            *(view(r, k, b) for r, k in zip(near_in, kinds_in)),
            *(view(r, k, b) for r, k in zip(near_out, kinds_out)),
            *scratch,
        )
        for copy in copies(far_out, buffers_out, moved_out, sem_out, b, False, True):
            copy.start()
        return 0

    lax.fori_loop(0, steps, step, 0)
    if end is not None:
        end(*near_in, *near_out, *scratch)
    for copy in copies(far_out, buffers_out, moved_out, sem_out, 0, True, True):
        copy.start()
    for b in range(steps):
        for whole in (True, False) if b == 0 else (False,):
            for copy in copies(far_out, buffers_out, moved_out, sem_out, b, whole, True):
                copy.wait()


def call(kernel, steps, ins, outs, scratch, flops, begin=None, end=None):
    arrays = [e[0] if e[2:] else pltpu.with_memory_space_constraint(e[0], pltpu.HBM) for e in ins]
    buffers = [(e[0].shape, e[0].dtype) for e in ins if not e[2:]] + [e[0] for e in outs if not e[2:]]
    moved = sum(a.size * a.dtype.itemsize for a in arrays)
    moved += sum(int(np.prod(e[0][0])) * jnp.dtype(e[0][1]).itemsize for e in outs)
    far = pl.BlockSpec(memory_space=pltpu.HBM)
    near = pl.BlockSpec(memory_space=pltpu.VMEM)
    kinds = [(None, *e[1:]) for e in ins]
    return pl.pallas_call(
        functools.partial(streamed, kernel, begin, end, steps, kinds, outs),
        in_specs=[near if e[2:] else far for e in ins],
        out_specs=[near if e[2:] else far for e in outs],
        out_shape=[jax.ShapeDtypeStruct(*e[0]) if e[2:] else pltpu.HBM(*e[0]) for e in outs],
        scratch_shapes=[pltpu.VMEM(s, d) for s, d in buffers]
        + scratch
        + [pltpu.SemaphoreType.DMA((steps, len(ins))), pltpu.SemaphoreType.DMA((steps, len(outs)))],
        compiler_params=pltpu.CompilerParams(vmem_limit_bytes=24 * MIB),
        cost_estimate=pl.CostEstimate(flops=flops, bytes_accessed=moved, transcendentals=0),
    )(*arrays)


def shards(q_stream, k_stream, v_stream, out_grad, norm_gain, residue, rate):
    count = lax.axis_size("ctx")
    _, length, channels = q_stream.shape
    seq_len = length * count
    modes = residue.shape[1]
    model_width = float(channels * lax.axis_size("chan"))
    chunk = math.gcd(length, 64)
    chunks = length // chunk
    groups = channels // LANES
    width = min(channels, 512)
    grid = channels // width
    broad = min(channels, 1024)
    q, k, v, og = (x[0] for x in (q_stream, k_stream, v_stream, out_grad))
    res = residue.T
    gain = norm_gain[None]
    full = fourier(chunk)
    basis = [terms(full, ["hl"]), terms(full, ["hhl"]), terms(full.T / np.float32(chunk), ["hh", "l0"])]
    basis = [(x, None) for x in basis]

    def inputs(*arrays, width=width):
        return [(a, (a.ndim - 1, width)) for a in arrays]

    def outputs(*shapes_types, width=width):
        return [(((*s, channels), d), (len(s), width)) for s, d in shapes_types]

    def held_inputs(*arrays, width=width):
        return [(a, (a.ndim - 1, width), True) for a in arrays]

    unit = 2 * length * channels * modes
    send = ((count, modes), BF16)
    states = ((chunks, modes), F32)
    held = pltpu.VMEM((width // LANES, chunks * modes, LANES), F32)

    vals, lam, parts, state = call(
        functools.partial(state_kernel, float(seq_len), chunk), grid, inputs(k, v, rate.T),
        outputs(((length,), BF16), ((modes,), F32), states, send), [], unit,
    )
    pieces = lax.all_to_all(state, "ctx", 0, 0)
    conv_local, ks, slopes, slope = call(
        functools.partial(local_kernel, chunk), channels // broad, inputs(vals, lam, res, parts, width=broad) + basis,
        outputs(((length,), F32), ((2 * chunk,), F32), states, ((modes,), F32), width=broad),
        [pltpu.VMEM((chunk, broad), F32)], 8 * unit,
    )
    conv, sums, carried, moved = call(
        functools.partial(forward_kernel, chunk), grid,
        held_inputs(lam, res, parts) + inputs(conv_local) + held_inputs(gain, pieces, q, og),
        [(((length, channels), F32), (1, width), True), (((2, length), F32), None, True)]
        + outputs(states, ((modes,), F32)),
        [held, pltpu.VMEM((2, length, LANES), F32)], unit, forward_begin, forward_end,
    )
    peers = lax.ppermute(sums, "chan", [(0, 1), (1, 0)])
    y_out, grad_q, gate, gain_part, gw, state = call(
        functools.partial(gate_kernel, chunk), grid,
        held_inputs(lam, gain) + [(sums, None, True), (peers, None, True)] + held_inputs(conv, q, og),
        outputs(((length,), BF16), ((length,), BF16), ((length,), F32), ((1,), F32), states, send),
        [pltpu.VMEM((length, LANES), F32)] * 2, unit, functools.partial(gate_begin, model_width),
    )
    later = lax.all_to_all(state, "ctx", 0, 0)
    rows = 2 * modes + ROWS
    grads_shape = (groups, rows, LANES)
    vg_local, grads = call(
        functools.partial(backward_kernel, chunk), grid,
        inputs(lam, gate, vals, ks, carried, moved, slopes, gw, gain_part) + basis,
        outputs(((length,), F32)) + [((grads_shape, F32), (0, width // LANES))],
        [pltpu.VMEM((chunk, width), F32)], 8 * unit,
    )
    adj, grads = call(
        functools.partial(adjoint_kernel, float(length)), 1,
        [(grads, (0, groups))] + [(a, None, True) for a in (lam, res, slope, later)],
        [((lam.shape, F32), (1, channels)), ((grads_shape, BF16), (0, groups))], [], channels * modes * 40,
    )
    grad_k, grad_v = call(
        functools.partial(finish_kernel, chunk), grid, inputs(adj) + held_inputs(lam, res) + inputs(gw, vg_local) + held_inputs(k, v),
        outputs(((length,), BF16), ((length,), BF16)), [held], unit,
    )
    both = ("ctx", "dp")
    if count * lax.axis_size("dp") == groups:
        parts = lax.all_to_all(grads, both, 0, 0)
        mine = jnp.sum(parts.astype(F32), axis=0).astype(BF16)
        total = lax.all_to_all(jnp.broadcast_to(mine[None], grads.shape), both, 0, 0).astype(F32)
    else:
        total = lax.psum(grads.astype(F32), both)
    by_mode = total.transpose(1, 0, 2).reshape(rows, channels)
    return (
        y_out[None],
        grad_q[None],
        grad_k[None],
        grad_v[None],
        by_mode[:modes].T,
        by_mode[modes : 2 * modes].T,
        by_mode[2 * modes],
    )


def solution(mesh):
    streams = P("dp", "ctx", "chan")
    in_specs = (streams,) * 4 + (P("chan"), P("chan", None), P("chan", None))
    out_specs = (streams,) * 4 + (P("chan", None), P("chan", None), P("chan"))
    return jax.shard_map(shards, mesh=mesh, in_specs=in_specs, out_specs=out_specs, check_vma=False)
```

```python
import functools
import math

import jax
import jax.numpy as jnp
import numpy as np
from jax import lax
from jax.experimental import pallas as pl
from jax.experimental.pallas import tpu as pltpu
from jax.sharding import PartitionSpec as P

EPSILON = 1e-06
LANES = 128
ROWS = 8
F32 = jnp.float32
BF16 = jnp.bfloat16
MIB = 1024 * 1024


def fourier(length):
    freq = 2 * np.arange(length)[:, None] + 1
    phase = (freq * np.arange(length)[None, :]) % (4 * length) * (2.0 * np.pi / (4 * length))
    return np.concatenate([np.cos(phase), -np.sin(phase)], axis=0).astype(np.float32)


def terms(full, order):
    high = full.astype(jnp.bfloat16)
    low = (full - high.astype(np.float32)).astype(jnp.bfloat16)
    pick = {"h": high, "l": low, "0": np.zeros_like(high)}
    return jnp.asarray(np.block([[pick[o] for o in row] for row in order]))


def triple(x):
    high = x.astype(BF16)
    low = (x - high.astype(F32)).astype(BF16)
    return jnp.concatenate([high, low, high], axis=0)


def inverse(t_ref, x):
    high = x.astype(BF16)
    low = (x - high.astype(F32)).astype(BF16)
    both = dot(t_ref[...], jnp.concatenate([high, low], axis=0))
    half = both.shape[0] // 2
    return both[:half] + both[half:]


def dot(a, b):
    return jnp.dot(a, b, preferred_element_type=F32)


def spread(ref, cols, first=0, count=16):
    return jnp.stack(
        [jnp.broadcast_to(ref[m : m + 1, cols], (ROWS, LANES)) for m in range(first, first + count)]
    )


def sublane():
    return lax.broadcasted_iota(jnp.int32, (ROWS, LANES), 0)


def fold(x):
    row = sublane()
    out = []
    for m in range(0, x.shape[0], ROWS):
        regs = [x[m + r] for r in range(ROWS)]
        for half in (4, 2, 1):
            low = (row & half) == 0
            regs = [
                jnp.where(
                    low,
                    regs[r] + pltpu.roll(regs[r], ROWS - half, 0),
                    regs[r + half] + pltpu.roll(regs[r + half], half, 0),
                )
                for r in range(half)
            ]
        out.append(regs[0])
    return jnp.concatenate(out, axis=0)


def fold_rounded(x):
    modes = x.shape[0]
    flat = x.reshape(modes * ROWS, LANES).astype(BF16)
    own = lax.broadcasted_iota(jnp.int32, (modes, modes * ROWS), 1) // ROWS
    pick = (own == lax.broadcasted_iota(jnp.int32, own.shape, 0)).astype(F32).astype(BF16)
    return dot(pick, flat)


def groups_of(width, body):
    def step(i, _):
        body(i, pl.ds(pl.multiple_of(i * LANES, LANES), LANES))
        return 0

    lax.fori_loop(0, width // LANES, step, 0, unroll=UNROLL)


UNROLL = True


def evaluate(start, step, tiles):
    term = start
    for i in range(tiles):
        yield jnp.sum(term, axis=0)
        if i + 1 < tiles:
            term = term * step


def gather_states(pieces_ref, cols, decay_block, forward):
    rank = lax.axis_index("ctx")
    count = pieces_ref.shape[0]
    total = jnp.zeros_like(decay_block)
    slope = jnp.zeros_like(decay_block)
    for s in range(count) if forward else range(count - 1, -1, -1):
        inside = (s < rank) if forward else (s > rank)
        piece = pieces_ref[s, :, cols].astype(F32)
        if forward:
            slope = jnp.where(inside, decay_block * (slope + total), slope)
        total = jnp.where(inside, decay_block * total + piece, total)
    return total, slope


def state_kernel(seq_len, chunk, k_ref, v_ref, rate_ref, val_ref, lam_ref, parts_ref, send_ref):
    length, width = k_ref.shape

    def body(i, cols):
        lam_rows = jnp.exp(rate_ref[:, cols]) * (1.0 / seq_len)
        lam_ref[:, cols] = lam_rows
        lam = spread(lam_ref, cols)
        step = jnp.exp(-ROWS * lam)
        weight = jnp.exp(-lam * (ROWS - 1 - sublane()).astype(F32))
        decay_chunk = jnp.exp(-float(chunk) * lam_rows)
        total = None
        for c in range(length // chunk):
            acc = None
            for a in range(c * chunk, (c + 1) * chunk, 16):
                rows = slice(a, a + 16)
                vals = k_ref[rows, cols] * v_ref[rows, cols]
                val_ref[rows, cols] = vals
                vals = vals.astype(F32)
                for tile in (vals[:ROWS], vals[ROWS:]):
                    acc = acc * step + tile[None] if acc is not None else jnp.broadcast_to(tile[None], lam.shape)
            part = fold_rounded(acc * weight)
            parts_ref[c, :, cols] = part
            total = part if total is None else total * decay_chunk + part
        for dest in range(send_ref.shape[0]):
            send_ref[dest, :, cols] = total.astype(BF16)

    groups_of(width, body)


def local_kernel(chunk, val_ref, lam_ref, res_ref, parts_ref, fv_ref, fa_ref, ta_ref,
                 conv_ref, ks_ref, slopes_ref, slope_ref, ker):
    length, width = val_ref.shape

    def body(i, cols):
        lam = spread(lam_ref, cols)
        step = jnp.exp(-ROWS * lam)
        row = sublane().astype(F32)
        start = spread(res_ref, cols) * jnp.exp(-lam * row)
        for a, tile in enumerate(evaluate(start, step, chunk // ROWS)):
            ker[a * ROWS : (a + 1) * ROWS, cols] = tile
        weight = jnp.exp(-lam * (ROWS - 1 - row))
        decay_chunk = jnp.exp(-float(chunk) * lam_ref[:, cols])
        total = slope = jnp.zeros_like(decay_chunk)
        for c in range(length // chunk):
            acc = None
            for a in range(0, chunk, 16):
                vals = val_ref[c * chunk + a : c * chunk + a + 16, cols].astype(F32)
                for h in (0, ROWS):
                    tile = (vals[h : h + ROWS] * (float(chunk - 1 - a - h) - row))[None]
                    acc = acc * step + tile if acc is not None else jnp.broadcast_to(tile, lam.shape)
            part = fold(acc * weight)
            slopes_ref[c, :, cols] = part
            slope = decay_chunk * (slope + float(chunk) * total) + part
            total = decay_chunk * total + parts_ref[c, :, cols]
        slope_ref[:, cols] = slope

    groups_of(width, body)
    ks = dot(fa_ref[...], triple(ker[...]))
    ks_ref[...] = ks
    kr, ki = ks[:chunk], ks[chunk:]
    for a in range(0, length, chunk):
        vals = val_ref[a : a + chunk]
        vs = dot(fv_ref[...], jnp.concatenate([vals, vals], axis=0))
        vr, vi = vs[:chunk], vs[chunk:]
        prod = jnp.concatenate([vr * kr - vi * ki, vr * ki + vi * kr], axis=0)
        conv_ref[a : a + chunk] = inverse(ta_ref, prod)


def forward_begin(*refs):
    acc_ref = refs[-1]
    acc_ref[...] = jnp.zeros_like(acc_ref)


def forward_end(*refs):
    sums_ref, acc_ref = refs[9], refs[-1]
    for n in range(2):
        sums_ref[n : n + 1] = jnp.sum(acc_ref[n].T, axis=0, keepdims=True)


def forward_kernel(chunk, lam_ref, res_ref, parts_ref, conv_in_ref, gain_ref, pieces_ref, q_ref, og_ref,
                   conv_ref, sums_ref, states_ref, moved_ref, held, acc_ref):
    length, width = q_ref.shape

    def body(i, cols):
        lam_rows = lam_ref[:, cols]
        modes = lam_rows.shape[0]
        state, moved = gather_states(pieces_ref, cols, jnp.exp(-float(length) * lam_rows), True)
        moved_ref[:, cols] = moved * float(length)
        decay_chunk = jnp.exp(-float(chunk) * lam_rows)
        res = res_ref[:, cols]
        for c in range(length // chunk):
            states_ref[c, :, cols] = state
            held[i, c * modes : (c + 1) * modes] = state * res
            state = decay_chunk * state + parts_ref[c, :, cols]
        lam = spread(lam_ref, cols)
        step = jnp.exp(-ROWS * lam)
        weight = jnp.exp(-lam * (sublane() + 1).astype(F32))
        gain = gain_ref[:, cols]
        for c in range(length // chunk):
            start = spread(held.at[i], slice(None), c * modes, modes) * weight
            tiles = evaluate(start, step, chunk // ROWS)
            for a in range(c * chunk, (c + 1) * chunk, 16):
                rows = slice(a, a + 16)
                conv = conv_in_ref[rows, cols] + jnp.concatenate([next(tiles), next(tiles)], axis=0)
                conv_ref[rows, cols] = conv
                mixed = q_ref[rows, cols].astype(F32) * conv
                scaled = gain * og_ref[rows, cols].astype(F32)
                acc_ref[0, rows] += mixed * mixed
                acc_ref[1, rows] += scaled * mixed

    groups_of(width, body)


def gate_begin(model_width, lam_ref, gain_ref, sums_ref, peer_ref, *refs):
    inv_ref, coef_ref = refs[-2:]
    squares = sums_ref[0:1] + peer_ref[0:1]
    inner = sums_ref[1:2] + peer_ref[1:2]
    inv = lax.rsqrt(squares / model_width + EPSILON)
    coef = inv * inv * inv * inner / model_width
    for row, ref in ((inv, inv_ref), (coef, coef_ref)):
        ref[...] = jnp.broadcast_to(row, (LANES, row.shape[1])).T


def gate_kernel(chunk, lam_ref, gain_ref, sums_ref, peer_ref, conv_ref, q_ref, og_ref,
                y_ref, gq_ref, gate_ref, gain_part_ref, gw_ref, send_ref, inv_ref, coef_ref):
    length, width = q_ref.shape

    def body(i, cols):
        lam = spread(lam_ref, cols)
        step = jnp.exp(-ROWS * lam)
        weight = jnp.exp(-lam * (sublane() + 1).astype(F32))
        decay_chunk = jnp.exp(-float(chunk) * lam_ref[:, cols])
        gain = gain_ref[:, cols]
        gain_acc = jnp.zeros((16, LANES), F32)
        total = None
        for c in range(length // chunk - 1, -1, -1):
            acc = None
            for a in range((c + 1) * chunk - 16, c * chunk - 1, -16):
                rows = slice(a, a + 16)
                inv = inv_ref[rows]
                q = q_ref[rows, cols].astype(F32)
                og = og_ref[rows, cols].astype(F32)
                conv = conv_ref[rows, cols]
                mixed = q * conv
                normed = mixed * inv
                y_ref[rows, cols] = (gain * normed).astype(BF16)
                gain_acc = gain_acc + og * normed
                mixed_grad = inv * (gain * og) - mixed * coef_ref[rows]
                gq_ref[rows, cols] = (mixed_grad * conv).astype(BF16)
                gate = mixed_grad * q
                gate_ref[rows, cols] = gate
                for tile in (gate[ROWS:], gate[:ROWS]):
                    acc = acc * step + tile[None] if acc is not None else jnp.broadcast_to(tile[None], lam.shape)
            part = fold_rounded(acc * weight)
            gw_ref[c, :, cols] = part
            total = part if total is None else total * decay_chunk + part
        gain_part_ref[:, cols] = jnp.sum(gain_acc, axis=0, keepdims=True)
        for dest in range(send_ref.shape[0]):
            send_ref[dest, :, cols] = total.astype(BF16)

    groups_of(width, body)


def backward_kernel(chunk, lam_ref, gate_ref, val_ref, ks_ref, states_ref, moved_ref, slopes_ref, gw_ref,
                    gain_part_ref, fv_ref, fa_ref, ta_ref, vg_ref, grads_ref, kg):
    length, width = gate_ref.shape
    kr, ki = ks_ref[:chunk], ks_ref[chunk:]
    cross_r = cross_i = None
    for a in range(0, length, chunk):
        gs = dot(fa_ref[...], triple(gate_ref[a : a + chunk]))
        gr, gi = gs[:chunk], gs[chunk:]
        vals = val_ref[a : a + chunk]
        vs = dot(fv_ref[...], jnp.concatenate([vals, vals], axis=0))
        vr, vi = vs[:chunk], vs[chunk:]
        real, imag = gr * vr + gi * vi, gi * vr - gr * vi
        cross_r = real if cross_r is None else cross_r + real
        cross_i = imag if cross_i is None else cross_i + imag
        prod = jnp.concatenate([gr * kr + gi * ki, gi * kr - gr * ki], axis=0)
        vg_ref[a : a + chunk] = inverse(ta_ref, prod)
    kg[...] = inverse(ta_ref, jnp.concatenate([cross_r, cross_i], axis=0))

    def body(i, cols):
        lam_rows = lam_ref[:, cols]
        modes = lam_rows.shape[0]
        lam = spread(lam_ref, cols)
        row = sublane().astype(F32)
        step = jnp.exp(-ROWS * lam)
        acc_r = acc_s = jnp.zeros_like(lam)
        for a in range(chunk - ROWS, -1, -ROWS):
            tile = kg[a : a + ROWS, cols]
            acc_r = acc_r * step + tile[None]
            acc_s = acc_s * step + (tile * (row + float(a)))[None]
        weight = jnp.exp(-lam * row)
        total_r = fold(acc_r * weight)
        total_s = fold(acc_s * weight)
        weight = jnp.exp(-lam * (row + 1.0))
        decay_chunk = jnp.exp(-float(chunk) * lam_rows)
        slope = moved_ref[:, cols]
        for c in range(length // chunk):
            acc = None
            for a in range(chunk - ROWS, -1, -ROWS):
                tile = gate_ref[c * chunk + a : c * chunk + a + ROWS, cols] * (row + float(a + 1))
                acc = acc * step + tile[None] if acc is not None else jnp.broadcast_to(tile[None], lam.shape)
            g_one = fold(acc * weight)
            state = states_ref[c, :, cols]
            gw = gw_ref[c, :, cols]
            total_r = total_r + gw * state
            total_s = total_s + g_one * state + gw * slope
            slope = decay_chunk * (slope + float(chunk) * state) + slopes_ref[c, :, cols]
        grads_ref[i, :modes] = total_r
        grads_ref[i, modes : 2 * modes] = total_s
        grads_ref[i, 2 * modes :] = jnp.broadcast_to(gain_part_ref[:, cols], (ROWS, LANES))

    groups_of(width, body)


def adjoint_kernel(length, grads_ref, lam_ref, res_ref, slope_ref, pieces_ref, adj_ref, out_ref):
    modes, width = lam_ref.shape

    def body(i, cols):
        lam = lam_ref[:, cols]
        total, _ = gather_states(pieces_ref, cols, jnp.exp(-length * lam), False)
        adj_ref[:, cols] = total
        out_ref[i, :modes] = grads_ref[i, :modes].astype(BF16)
        total_s = grads_ref[i, modes : 2 * modes] + slope_ref[:, cols] * total
        out_ref[i, modes : 2 * modes] = (-lam * res_ref[:, cols] * total_s).astype(BF16)
        out_ref[i, 2 * modes :] = grads_ref[i, 2 * modes :].astype(BF16)

    groups_of(width, body)


def finish_kernel(chunk, adj_ref, lam_ref, res_ref, gw_ref, vg_ref, k_ref, v_ref, gk_ref, gv_ref, held):
    length, width = k_ref.shape

    def body(i, cols):
        lam_rows = lam_ref[:, cols]
        modes = lam_rows.shape[0]
        decay_chunk = jnp.exp(-float(chunk) * lam_rows)
        adj = adj_ref[:, cols]
        res = res_ref[:, cols]
        for c in range(length // chunk - 1, -1, -1):
            held[i, c * modes : (c + 1) * modes] = adj * res
            adj = decay_chunk * adj + gw_ref[c, :, cols]
        lam = spread(lam_ref, cols)
        step = jnp.exp(-ROWS * lam)
        weight = jnp.exp(-lam * (ROWS - 1 - sublane()).astype(F32))
        for c in range(length // chunk - 1, -1, -1):
            start = spread(held.at[i], slice(None), c * modes, modes) * weight
            tiles = evaluate(start, step, chunk // ROWS)
            for a in range((c + 1) * chunk - 16, c * chunk - 1, -16):
                rows = slice(a, a + 16)
                upper = next(tiles)
                grad = vg_ref[rows, cols] + jnp.concatenate([next(tiles), upper], axis=0)
                gk_ref[rows, cols] = (grad * v_ref[rows, cols].astype(F32)).astype(BF16)
                gv_ref[rows, cols] = (grad * k_ref[rows, cols].astype(F32)).astype(BF16)

    groups_of(width, body)


def streamed(body, begin, end, steps, kinds_in, kinds_out, *refs):
    ins, refs = refs[: len(kinds_in)], refs[len(kinds_in) :]
    outs, refs = refs[: len(kinds_out)], refs[len(kinds_out) :]

    def buffered(arrays, kinds, refs):
        away = [n for n, kind in enumerate(kinds) if not kind[2:]]
        near = list(arrays)
        for n, buffer in zip(away, refs):
            near[n] = buffer
        far = [arrays[n] for n in away]
        return near, far, refs[: len(away)], [kinds[n][1] for n in away], refs[len(away) :]

    near_in, far_in, buffers_in, moved_in, refs = buffered(ins, kinds_in, refs)
    near_out, far_out, buffers_out, moved_out, refs = buffered(outs, kinds_out, refs)
    kinds_in, kinds_out = [kind[1] for kind in kinds_in], [kind[1] for kind in kinds_out]
    scratch, (sem_in, sem_out) = refs[:-2], refs[-2:]

    def view(ref, kind, b):
        if kind is None:
            return ref
        axis, size = kind
        start = b * size if axis == 0 else pl.multiple_of(b * size, LANES)
        return ref.at[(slice(None),) * axis + (pl.ds(start, size),)]

    def copies(far, near, kinds, sem, b, whole, outward):
        for n, kind in enumerate(kinds):
            if (kind is None) == whole:
                pair = view(far[n], kind, b), view(near[n], kind, b)
                source, target = pair[::-1] if outward else pair
                yield pltpu.make_async_copy(source, target, sem.at[b, n])

    for b in range(steps):
        for whole in (True, False) if b == 0 else (False,):
            for copy in copies(far_in, buffers_in, moved_in, sem_in, b, whole, False):
                copy.start()
    for copy in copies(far_in, buffers_in, moved_in, sem_in, 0, True, False):
        copy.wait()
    if begin is not None:
        begin(*near_in, *near_out, *scratch)

    def step(b, _):
        for copy in copies(far_in, buffers_in, moved_in, sem_in, b, False, False):
            copy.wait()
        body(
            *(view(r, k, b) for r, k in zip(near_in, kinds_in)),
            *(view(r, k, b) for r, k in zip(near_out, kinds_out)),
            *scratch,
        )
        for copy in copies(far_out, buffers_out, moved_out, sem_out, b, False, True):
            copy.start()
        return 0

    lax.fori_loop(0, steps, step, 0)
    if end is not None:
        end(*near_in, *near_out, *scratch)
    for copy in copies(far_out, buffers_out, moved_out, sem_out, 0, True, True):
        copy.start()
    for b in range(steps):
        for whole in (True, False) if b == 0 else (False,):
            for copy in copies(far_out, buffers_out, moved_out, sem_out, b, whole, True):
                copy.wait()


def call(kernel, steps, ins, outs, scratch, flops, begin=None, end=None):
    arrays = [e[0] if e[2:] else pltpu.with_memory_space_constraint(e[0], pltpu.HBM) for e in ins]
    buffers = [(e[0].shape, e[0].dtype) for e in ins if not e[2:]] + [e[0] for e in outs if not e[2:]]
    moved = sum(a.size * a.dtype.itemsize for a in arrays)
    moved += sum(int(np.prod(e[0][0])) * jnp.dtype(e[0][1]).itemsize for e in outs)
    far = pl.BlockSpec(memory_space=pltpu.HBM)
    near = pl.BlockSpec(memory_space=pltpu.VMEM)
    kinds = [(None, *e[1:]) for e in ins]
    return pl.pallas_call(
        functools.partial(streamed, kernel, begin, end, steps, kinds, outs),
        in_specs=[near if e[2:] else far for e in ins],
        out_specs=[near if e[2:] else far for e in outs],
        out_shape=[jax.ShapeDtypeStruct(*e[0]) if e[2:] else pltpu.HBM(*e[0]) for e in outs],
        scratch_shapes=[pltpu.VMEM(s, d) for s, d in buffers]
        + scratch
        + [pltpu.SemaphoreType.DMA((steps, len(ins))), pltpu.SemaphoreType.DMA((steps, len(outs)))],
        compiler_params=pltpu.CompilerParams(vmem_limit_bytes=24 * MIB),
        cost_estimate=pl.CostEstimate(flops=flops, bytes_accessed=moved, transcendentals=0),
    )(*arrays)


def shards(q_stream, k_stream, v_stream, out_grad, norm_gain, residue, rate):
    count = lax.axis_size("ctx")
    _, length, channels = q_stream.shape
    seq_len = length * count
    modes = residue.shape[1]
    model_width = float(channels * lax.axis_size("chan"))
    chunk = math.gcd(length, 64)
    chunks = length // chunk
    groups = channels // LANES
    width = min(channels, 512)
    grid = channels // width
    broad = min(channels, 1024)
    q, k, v, og = (x[0] for x in (q_stream, k_stream, v_stream, out_grad))
    res = residue.T
    gain = norm_gain[None]
    full = fourier(chunk)
    basis = [terms(full, ["hl"]), terms(full, ["hhl"]), terms(full.T / np.float32(chunk), ["hh", "l0"])]
    basis = [(x, None) for x in basis]

    def inputs(*arrays, width=width):
        return [(a, (a.ndim - 1, width)) for a in arrays]

    def outputs(*shapes_types, width=width):
        return [(((*s, channels), d), (len(s), width)) for s, d in shapes_types]

    def held_inputs(*arrays, width=width):
        return [(a, (a.ndim - 1, width), True) for a in arrays]

    unit = 2 * length * channels * modes
    send = ((count, modes), BF16)
    states = ((chunks, modes), F32)
    held = pltpu.VMEM((width // LANES, chunks * modes, LANES), F32)

    vals, lam, parts, state = call(
        functools.partial(state_kernel, float(seq_len), chunk), grid, inputs(k, v, rate.T),
        outputs(((length,), BF16), ((modes,), F32), states, send), [], unit,
    )
    pieces = lax.all_to_all(state, "ctx", 0, 0)
    conv_local, ks, slopes, slope = call(
        functools.partial(local_kernel, chunk), channels // broad, inputs(vals, lam, res, parts, width=broad) + basis,
        outputs(((length,), F32), ((2 * chunk,), F32), states, ((modes,), F32), width=broad),
        [pltpu.VMEM((chunk, broad), F32)], 8 * unit,
    )
    conv, sums, carried, moved = call(
        functools.partial(forward_kernel, chunk), grid,
        held_inputs(lam, res, parts) + inputs(conv_local) + held_inputs(gain, pieces, q, og),
        [(((length, channels), F32), (1, width), True), (((2, length), F32), None, True)]
        + outputs(states, ((modes,), F32)),
        [held, pltpu.VMEM((2, length, LANES), F32)], unit, forward_begin, forward_end,
    )
    peers = lax.ppermute(sums, "chan", [(0, 1), (1, 0)])
    y_out, grad_q, gate, gain_part, gw, state = call(
        functools.partial(gate_kernel, chunk), grid,
        held_inputs(lam, gain) + [(sums, None, True), (peers, None, True)] + held_inputs(conv, q, og),
        outputs(((length,), BF16), ((length,), BF16), ((length,), F32), ((1,), F32), states, send),
        [pltpu.VMEM((length, LANES), F32)] * 2, unit, functools.partial(gate_begin, model_width),
    )
    later = lax.all_to_all(state, "ctx", 0, 0)
    rows = 2 * modes + ROWS
    grads_shape = (groups, rows, LANES)
    vg_local, grads = call(
        functools.partial(backward_kernel, chunk), grid,
        inputs(lam, gate, vals, ks, carried, moved, slopes, gw, gain_part) + basis,
        outputs(((length,), F32)) + [((grads_shape, F32), (0, width // LANES))],
        [pltpu.VMEM((chunk, width), F32)], 8 * unit,
    )
    adj, grads = call(
        functools.partial(adjoint_kernel, float(length)), 1,
        [(grads, (0, groups))] + [(a, None, True) for a in (lam, res, slope, later)],
        [((lam.shape, F32), (1, channels)), ((grads_shape, BF16), (0, groups))], [], channels * modes * 40,
    )
    grad_k, grad_v = call(
        functools.partial(finish_kernel, chunk), grid, inputs(adj) + held_inputs(lam, res) + inputs(gw, vg_local) + held_inputs(k, v),
        outputs(((length,), BF16), ((length,), BF16)), [held], unit,
    )
    both = ("ctx", "dp")
    if count * lax.axis_size("dp") == groups:
        parts = lax.all_to_all(grads, both, 0, 0)
        mine = jnp.sum(parts.astype(F32), axis=0).astype(BF16)
        total = lax.all_to_all(jnp.broadcast_to(mine[None], grads.shape), both, 0, 0).astype(F32)
    else:
        total = lax.psum(grads.astype(F32), both)
    by_mode = total.transpose(1, 0, 2).reshape(rows, channels)
    return (
        y_out[None],
        grad_q[None],
        grad_k[None],
        grad_v[None],
        by_mode[:modes].T,
        by_mode[modes : 2 * modes].T,
        by_mode[2 * modes],
    )


def solution(mesh):
    streams = P("dp", "ctx", "chan")
    in_specs = (streams,) * 4 + (P("chan"), P("chan", None), P("chan", None))
    out_specs = (streams,) * 4 + (P("chan", None), P("chan", None), P("chan"))
    return jax.shard_map(shards, mesh=mesh, in_specs=in_specs, out_specs=out_specs, check_vma=False)
```

```python
import functools
import math

import jax
import jax.numpy as jnp
import numpy as np
from jax import lax
from jax.experimental import pallas as pl
from jax.experimental.pallas import tpu as pltpu
from jax.sharding import PartitionSpec as P

EPSILON = 1e-06
LANES = 128
ROWS = 8
F32 = jnp.float32
BF16 = jnp.bfloat16
MIB = 1024 * 1024


def fourier(length):
    freq = 2 * np.arange(length)[:, None] + 1
    phase = (freq * np.arange(length)[None, :]) % (4 * length) * (2.0 * np.pi / (4 * length))
    return np.concatenate([np.cos(phase), -np.sin(phase)], axis=0).astype(np.float32)


def terms(full, order):
    high = full.astype(jnp.bfloat16)
    low = (full - high.astype(np.float32)).astype(jnp.bfloat16)
    pick = {"h": high, "l": low, "0": np.zeros_like(high)}
    return jnp.asarray(np.block([[pick[o] for o in row] for row in order]))


def triple(x):
    high = x.astype(BF16)
    low = (x - high.astype(F32)).astype(BF16)
    return jnp.concatenate([high, low, high], axis=0)


def inverse(t_ref, x):
    high = x.astype(BF16)
    low = (x - high.astype(F32)).astype(BF16)
    both = dot(t_ref[...], jnp.concatenate([high, low], axis=0))
    half = both.shape[0] // 2
    return both[:half] + both[half:]


def dot(a, b):
    return jnp.dot(a, b, preferred_element_type=F32)


def spread(ref, cols, first=0, count=16):
    return jnp.stack(
        [jnp.broadcast_to(ref[m : m + 1, cols], (ROWS, LANES)) for m in range(first, first + count)]
    )


def sublane():
    return lax.broadcasted_iota(jnp.int32, (ROWS, LANES), 0)


def fold(x):
    row = sublane()
    out = []
    for m in range(0, x.shape[0], ROWS):
        regs = [x[m + r] for r in range(ROWS)]
        for half in (4, 2, 1):
            low = (row & half) == 0
            regs = [
                jnp.where(
                    low,
                    regs[r] + pltpu.roll(regs[r], ROWS - half, 0),
                    regs[r + half] + pltpu.roll(regs[r + half], half, 0),
                )
                for r in range(half)
            ]
        out.append(regs[0])
    return jnp.concatenate(out, axis=0)


def fold_rounded(x):
    modes = x.shape[0]
    flat = x.reshape(modes * ROWS, LANES).astype(BF16)
    own = lax.broadcasted_iota(jnp.int32, (modes, modes * ROWS), 1) // ROWS
    pick = (own == lax.broadcasted_iota(jnp.int32, own.shape, 0)).astype(F32).astype(BF16)
    return dot(pick, flat)


def groups_of(width, body):
    def step(i, _):
        body(i, pl.ds(pl.multiple_of(i * LANES, LANES), LANES))
        return 0

    lax.fori_loop(0, width // LANES, step, 0, unroll=UNROLL)


UNROLL = True


def evaluate(start, step, tiles):
    term = start
    for i in range(tiles):
        yield jnp.sum(term, axis=0)
        if i + 1 < tiles:
            term = term * step


def gather_states(pieces_ref, cols, decay_block, forward):
    rank = lax.axis_index("ctx")
    count = pieces_ref.shape[0]
    total = jnp.zeros_like(decay_block)
    slope = jnp.zeros_like(decay_block)
    for s in range(count) if forward else range(count - 1, -1, -1):
        inside = (s < rank) if forward else (s > rank)
        piece = pieces_ref[s, :, cols].astype(F32)
        if forward:
            slope = jnp.where(inside, decay_block * (slope + total), slope)
        total = jnp.where(inside, decay_block * total + piece, total)
    return total, slope


def state_kernel(seq_len, chunk, k_ref, v_ref, rate_ref, val_ref, lam_ref, parts_ref, send_ref):
    length, width = k_ref.shape

    def body(i, cols):
        lam_rows = jnp.exp(rate_ref[:, cols]) * (1.0 / seq_len)
        lam_ref[:, cols] = lam_rows
        lam = spread(lam_ref, cols)
        step = jnp.exp(-ROWS * lam)
        weight = jnp.exp(-lam * (ROWS - 1 - sublane()).astype(F32))
        decay_chunk = jnp.exp(-float(chunk) * lam_rows)
        total = None
        for c in range(length // chunk):
            acc = None
            for a in range(c * chunk, (c + 1) * chunk, 16):
                rows = slice(a, a + 16)
                vals = k_ref[rows, cols] * v_ref[rows, cols]
                val_ref[rows, cols] = vals
                vals = vals.astype(F32)
                for tile in (vals[:ROWS], vals[ROWS:]):
                    acc = acc * step + tile[None] if acc is not None else jnp.broadcast_to(tile[None], lam.shape)
            part = fold_rounded(acc * weight)
            parts_ref[c, :, cols] = part
            total = part if total is None else total * decay_chunk + part
        for dest in range(send_ref.shape[0]):
            send_ref[dest, :, cols] = total.astype(BF16)

    groups_of(width, body)


def local_kernel(chunk, val_ref, lam_ref, res_ref, parts_ref, fv_ref, fa_ref, ta_ref,
                 conv_ref, ks_ref, slopes_ref, slope_ref, ker):
    length, width = val_ref.shape

    def body(i, cols):
        lam = spread(lam_ref, cols)
        step = jnp.exp(-ROWS * lam)
        row = sublane().astype(F32)
        start = spread(res_ref, cols) * jnp.exp(-lam * row)
        for a, tile in enumerate(evaluate(start, step, chunk // ROWS)):
            ker[a * ROWS : (a + 1) * ROWS, cols] = tile
        weight = jnp.exp(-lam * (ROWS - 1 - row))
        decay_chunk = jnp.exp(-float(chunk) * lam_ref[:, cols])
        total = slope = jnp.zeros_like(decay_chunk)
        for c in range(length // chunk):
            acc = None
            for a in range(0, chunk, 16):
                vals = val_ref[c * chunk + a : c * chunk + a + 16, cols].astype(F32)
                for h in (0, ROWS):
                    tile = (vals[h : h + ROWS] * (float(chunk - 1 - a - h) - row))[None]
                    acc = acc * step + tile if acc is not None else jnp.broadcast_to(tile, lam.shape)
            part = fold(acc * weight)
            slopes_ref[c, :, cols] = part
            slope = decay_chunk * (slope + float(chunk) * total) + part
            total = decay_chunk * total + parts_ref[c, :, cols]
        slope_ref[:, cols] = slope

    groups_of(width, body)
    ks = dot(fa_ref[...], triple(ker[...]))
    ks_ref[...] = ks
    kr, ki = ks[:chunk], ks[chunk:]
    for a in range(0, length, chunk):
        vals = val_ref[a : a + chunk]
        vs = dot(fv_ref[...], jnp.concatenate([vals, vals], axis=0))
        vr, vi = vs[:chunk], vs[chunk:]
        prod = jnp.concatenate([vr * kr - vi * ki, vr * ki + vi * kr], axis=0)
        conv_ref[a : a + chunk] = inverse(ta_ref, prod)


def forward_begin(*refs):
    acc_ref = refs[-1]
    acc_ref[...] = jnp.zeros_like(acc_ref)


def forward_end(*refs):
    sums_ref, acc_ref = refs[9], refs[-1]
    for n in range(2):
        sums_ref[n : n + 1] = jnp.sum(acc_ref[n].T, axis=0, keepdims=True)


def forward_kernel(chunk, lam_ref, res_ref, parts_ref, conv_in_ref, gain_ref, pieces_ref, q_ref, og_ref,
                   conv_ref, sums_ref, states_ref, moved_ref, held, steps_ref, acc_ref):
    length, width = q_ref.shape

    def body(i, cols):
        lam_rows = lam_ref[:, cols]
        modes = lam_rows.shape[0]
        state, moved = gather_states(pieces_ref, cols, jnp.exp(-float(length) * lam_rows), True)
        moved_ref[:, cols] = moved * float(length)
        decay_chunk = jnp.exp(-float(chunk) * lam_rows)
        res = res_ref[:, cols]
        for c in range(length // chunk):
            states_ref[c, :, cols] = state
            held[i, c * modes : (c + 1) * modes] = state * res
            state = decay_chunk * state + parts_ref[c, :, cols]
        lam = spread(lam_ref, cols)
        steps_ref[i] = jnp.exp(-float(ROWS) * lam_ref[:, cols])
        step = spread(steps_ref.at[i], slice(None))
        weight = jnp.exp(-lam * (sublane() + 1).astype(F32))
        gain = gain_ref[:, cols]
        for c in range(length // chunk):
            start = spread(held.at[i], slice(None), c * modes, modes) * weight
            tiles = evaluate(start, step, chunk // ROWS)
            for a in range(c * chunk, (c + 1) * chunk, 16):
                rows = slice(a, a + 16)
                conv = conv_in_ref[rows, cols] + jnp.concatenate([next(tiles), next(tiles)], axis=0)
                conv_ref[rows, cols] = conv
                mixed = q_ref[rows, cols].astype(F32) * conv
                scaled = gain * og_ref[rows, cols].astype(F32)
                acc_ref[0, rows] += mixed * mixed
                acc_ref[1, rows] += scaled * mixed

    groups_of(width, body)


def gate_begin(model_width, lam_ref, gain_ref, sums_ref, peer_ref, *refs):
    inv_ref, coef_ref = refs[-2:]
    squares = sums_ref[0:1] + peer_ref[0:1]
    inner = sums_ref[1:2] + peer_ref[1:2]
    inv = lax.rsqrt(squares / model_width + EPSILON)
    coef = inv * inv * inv * inner / model_width
    for row, ref in ((inv, inv_ref), (coef, coef_ref)):
        ref[...] = jnp.broadcast_to(row, (LANES, row.shape[1])).T


def gate_kernel(chunk, lam_ref, gain_ref, sums_ref, peer_ref, conv_ref, q_ref, og_ref,
                y_ref, gq_ref, gate_ref, gain_part_ref, gw_ref, send_ref, inv_ref, coef_ref):
    length, width = q_ref.shape

    def body(i, cols):
        lam = spread(lam_ref, cols)
        weight = jnp.exp(-lam * (sublane() + 1).astype(F32))
        step = jnp.broadcast_to(weight[:, ROWS - 1 :], weight.shape)
        decay_chunk = jnp.exp(-float(chunk) * lam_ref[:, cols])
        gain = gain_ref[:, cols]
        gain_acc = jnp.zeros((16, LANES), F32)
        total = None
        for c in range(length // chunk - 1, -1, -1):
            acc = None
            for a in range((c + 1) * chunk - 16, c * chunk - 1, -16):
                rows = slice(a, a + 16)
                inv = inv_ref[rows]
                q = q_ref[rows, cols].astype(F32)
                og = og_ref[rows, cols].astype(F32)
                conv = conv_ref[rows, cols]
                mixed = q * conv
                normed = mixed * inv
                y_ref[rows, cols] = (gain * normed).astype(BF16)
                gain_acc = gain_acc + og * normed
                mixed_grad = inv * (gain * og) - mixed * coef_ref[rows]
                gq_ref[rows, cols] = (mixed_grad * conv).astype(BF16)
                gate = mixed_grad * q
                gate_ref[rows, cols] = gate
                for tile in (gate[ROWS:], gate[:ROWS]):
                    acc = acc * step + tile[None] if acc is not None else jnp.broadcast_to(tile[None], lam.shape)
            part = fold_rounded(acc * weight)
            gw_ref[c, :, cols] = part
            total = part if total is None else total * decay_chunk + part
        gain_part_ref[:, cols] = jnp.sum(gain_acc, axis=0, keepdims=True)
        for dest in range(send_ref.shape[0]):
            send_ref[dest, :, cols] = total.astype(BF16)

    groups_of(width, body)


def backward_kernel(chunk, lam_ref, gate_ref, val_ref, ks_ref, states_ref, moved_ref, slopes_ref, gw_ref,
                    gain_part_ref, fv_ref, fa_ref, ta_ref, vg_ref, grads_ref, kg):
    length, width = gate_ref.shape
    kr, ki = ks_ref[:chunk], ks_ref[chunk:]
    cross_r = cross_i = None
    for a in range(0, length, chunk):
        gs = dot(fa_ref[...], triple(gate_ref[a : a + chunk]))
        gr, gi = gs[:chunk], gs[chunk:]
        vals = val_ref[a : a + chunk]
        vs = dot(fv_ref[...], jnp.concatenate([vals, vals], axis=0))
        vr, vi = vs[:chunk], vs[chunk:]
        real, imag = gr * vr + gi * vi, gi * vr - gr * vi
        cross_r = real if cross_r is None else cross_r + real
        cross_i = imag if cross_i is None else cross_i + imag
        prod = jnp.concatenate([gr * kr + gi * ki, gi * kr - gr * ki], axis=0)
        vg_ref[a : a + chunk] = inverse(ta_ref, prod)
    kg[...] = inverse(ta_ref, jnp.concatenate([cross_r, cross_i], axis=0))

    def body(i, cols):
        lam_rows = lam_ref[:, cols]
        modes = lam_rows.shape[0]
        lam = spread(lam_ref, cols)
        row = sublane().astype(F32)
        step = jnp.exp(-ROWS * lam)
        acc_r = acc_s = jnp.zeros_like(lam)
        for a in range(chunk - ROWS, -1, -ROWS):
            tile = kg[a : a + ROWS, cols]
            acc_r = acc_r * step + tile[None]
            acc_s = acc_s * step + (tile * (row + float(a)))[None]
        weight = jnp.exp(-lam * row)
        total_r = fold(acc_r * weight)
        total_s = fold(acc_s * weight)
        weight = jnp.exp(-lam * (row + 1.0))
        decay_chunk = jnp.exp(-float(chunk) * lam_rows)
        slope = moved_ref[:, cols]
        for c in range(length // chunk):
            acc = None
            for a in range(chunk - ROWS, -1, -ROWS):
                tile = gate_ref[c * chunk + a : c * chunk + a + ROWS, cols] * (row + float(a + 1))
                acc = acc * step + tile[None] if acc is not None else jnp.broadcast_to(tile[None], lam.shape)
            g_one = fold(acc * weight)
            state = states_ref[c, :, cols]
            gw = gw_ref[c, :, cols]
            total_r = total_r + gw * state
            total_s = total_s + g_one * state + gw * slope
            slope = decay_chunk * (slope + float(chunk) * state) + slopes_ref[c, :, cols]
        grads_ref[i, :modes] = total_r
        grads_ref[i, modes : 2 * modes] = total_s
        grads_ref[i, 2 * modes :] = jnp.broadcast_to(gain_part_ref[:, cols], (ROWS, LANES))

    groups_of(width, body)


def adjoint_kernel(length, grads_ref, lam_ref, res_ref, slope_ref, pieces_ref, adj_ref, out_ref):
    modes, width = lam_ref.shape

    def body(i, cols):
        lam = lam_ref[:, cols]
        total, _ = gather_states(pieces_ref, cols, jnp.exp(-length * lam), False)
        adj_ref[:, cols] = total
        out_ref[i, :modes] = grads_ref[i, :modes].astype(BF16)
        total_s = grads_ref[i, modes : 2 * modes] + slope_ref[:, cols] * total
        out_ref[i, modes : 2 * modes] = (-lam * res_ref[:, cols] * total_s).astype(BF16)
        out_ref[i, 2 * modes :] = grads_ref[i, 2 * modes :].astype(BF16)

    groups_of(width, body)


def finish_kernel(chunk, adj_ref, lam_ref, res_ref, gw_ref, vg_ref, k_ref, v_ref, gk_ref, gv_ref, held):
    length, width = k_ref.shape

    def body(i, cols):
        lam_rows = lam_ref[:, cols]
        modes = lam_rows.shape[0]
        decay_chunk = jnp.exp(-float(chunk) * lam_rows)
        adj = adj_ref[:, cols]
        res = res_ref[:, cols]
        for c in range(length // chunk - 1, -1, -1):
            held[i, c * modes : (c + 1) * modes] = adj * res
            adj = decay_chunk * adj + gw_ref[c, :, cols]
        lam = spread(lam_ref, cols)
        step = jnp.exp(-ROWS * lam)
        weight = jnp.exp(-lam * (ROWS - 1 - sublane()).astype(F32))
        for c in range(length // chunk - 1, -1, -1):
            start = spread(held.at[i], slice(None), c * modes, modes) * weight
            tiles = evaluate(start, step, chunk // ROWS)
            for a in range((c + 1) * chunk - 16, c * chunk - 1, -16):
                rows = slice(a, a + 16)
                upper = next(tiles)
                grad = vg_ref[rows, cols] + jnp.concatenate([next(tiles), upper], axis=0)
                gk_ref[rows, cols] = (grad * v_ref[rows, cols].astype(F32)).astype(BF16)
                gv_ref[rows, cols] = (grad * k_ref[rows, cols].astype(F32)).astype(BF16)

    groups_of(width, body)


def streamed(body, begin, end, steps, kinds_in, kinds_out, *refs):
    ins, refs = refs[: len(kinds_in)], refs[len(kinds_in) :]
    outs, refs = refs[: len(kinds_out)], refs[len(kinds_out) :]

    def buffered(arrays, kinds, refs):
        away = [n for n, kind in enumerate(kinds) if not kind[2:]]
        near = list(arrays)
        for n, buffer in zip(away, refs):
            near[n] = buffer
        far = [arrays[n] for n in away]
        return near, far, refs[: len(away)], [kinds[n][1] for n in away], refs[len(away) :]

    near_in, far_in, buffers_in, moved_in, refs = buffered(ins, kinds_in, refs)
    near_out, far_out, buffers_out, moved_out, refs = buffered(outs, kinds_out, refs)
    kinds_in, kinds_out = [kind[1] for kind in kinds_in], [kind[1] for kind in kinds_out]
    scratch, (sem_in, sem_out) = refs[:-2], refs[-2:]

    def view(ref, kind, b):
        if kind is None:
            return ref
        axis, size = kind
        start = b * size if axis == 0 else pl.multiple_of(b * size, LANES)
        return ref.at[(slice(None),) * axis + (pl.ds(start, size),)]

    def copies(far, near, kinds, sem, b, whole, outward):
        for n, kind in enumerate(kinds):
            if (kind is None) == whole:
                pair = view(far[n], kind, b), view(near[n], kind, b)
                source, target = pair[::-1] if outward else pair
                yield pltpu.make_async_copy(source, target, sem.at[b, n])

    for b in range(steps):
        for whole in (True, False) if b == 0 else (False,):
            for copy in copies(far_in, buffers_in, moved_in, sem_in, b, whole, False):
                copy.start()
    for copy in copies(far_in, buffers_in, moved_in, sem_in, 0, True, False):
        copy.wait()
    if begin is not None:
        begin(*near_in, *near_out, *scratch)

    def step(b, _):
        for copy in copies(far_in, buffers_in, moved_in, sem_in, b, False, False):
            copy.wait()
        body(
            *(view(r, k, b) for r, k in zip(near_in, kinds_in)),
            *(view(r, k, b) for r, k in zip(near_out, kinds_out)),
            *scratch,
        )
        for copy in copies(far_out, buffers_out, moved_out, sem_out, b, False, True):
            copy.start()
        return 0

    lax.fori_loop(0, steps, step, 0)
    if end is not None:
        end(*near_in, *near_out, *scratch)
    for copy in copies(far_out, buffers_out, moved_out, sem_out, 0, True, True):
        copy.start()
    for b in range(steps):
        for whole in (True, False) if b == 0 else (False,):
            for copy in copies(far_out, buffers_out, moved_out, sem_out, b, whole, True):
                copy.wait()


def call(kernel, steps, ins, outs, scratch, flops, begin=None, end=None):
    arrays = [e[0] if e[2:] else pltpu.with_memory_space_constraint(e[0], pltpu.HBM) for e in ins]
    buffers = [(e[0].shape, e[0].dtype) for e in ins if not e[2:]] + [e[0] for e in outs if not e[2:]]
    moved = sum(a.size * a.dtype.itemsize for a in arrays)
    moved += sum(int(np.prod(e[0][0])) * jnp.dtype(e[0][1]).itemsize for e in outs)
    far = pl.BlockSpec(memory_space=pltpu.HBM)
    near = pl.BlockSpec(memory_space=pltpu.VMEM)
    kinds = [(None, *e[1:]) for e in ins]
    return pl.pallas_call(
        functools.partial(streamed, kernel, begin, end, steps, kinds, outs),
        in_specs=[near if e[2:] else far for e in ins],
        out_specs=[near if e[2:] else far for e in outs],
        out_shape=[jax.ShapeDtypeStruct(*e[0]) if e[2:] else pltpu.HBM(*e[0]) for e in outs],
        scratch_shapes=[pltpu.VMEM(s, d) for s, d in buffers]
        + scratch
        + [pltpu.SemaphoreType.DMA((steps, len(ins))), pltpu.SemaphoreType.DMA((steps, len(outs)))],
        compiler_params=pltpu.CompilerParams(vmem_limit_bytes=24 * MIB),
        cost_estimate=pl.CostEstimate(flops=flops, bytes_accessed=moved, transcendentals=0),
    )(*arrays)


def shards(q_stream, k_stream, v_stream, out_grad, norm_gain, residue, rate):
    count = lax.axis_size("ctx")
    _, length, channels = q_stream.shape
    seq_len = length * count
    modes = residue.shape[1]
    model_width = float(channels * lax.axis_size("chan"))
    chunk = math.gcd(length, 64)
    chunks = length // chunk
    groups = channels // LANES
    width = min(channels, 512)
    grid = channels // width
    broad = min(channels, 1024)
    q, k, v, og = (x[0] for x in (q_stream, k_stream, v_stream, out_grad))
    res = residue.T
    gain = norm_gain[None]
    full = fourier(chunk)
    basis = [terms(full, ["hl"]), terms(full, ["hhl"]), terms(full.T / np.float32(chunk), ["hh", "l0"])]
    basis = [(x, None) for x in basis]

    def inputs(*arrays, width=width):
        return [(a, (a.ndim - 1, width)) for a in arrays]

    def outputs(*shapes_types, width=width):
        return [(((*s, channels), d), (len(s), width)) for s, d in shapes_types]

    def held_inputs(*arrays, width=width):
        return [(a, (a.ndim - 1, width), True) for a in arrays]

    unit = 2 * length * channels * modes
    send = ((count, modes), BF16)
    states = ((chunks, modes), F32)
    steps = pltpu.VMEM((width // LANES, modes, LANES), F32)
    held = pltpu.VMEM((width // LANES, chunks * modes, LANES), F32)

    vals, lam, parts, state = call(
        functools.partial(state_kernel, float(seq_len), chunk), grid, inputs(k, v, rate.T),
        outputs(((length,), BF16), ((modes,), F32), states, send), [], unit,
    )
    pieces = lax.all_to_all(state, "ctx", 0, 0)
    conv_local, ks, slopes, slope = call(
        functools.partial(local_kernel, chunk), channels // broad, inputs(vals, lam, res, parts, width=broad) + basis,
        outputs(((length,), F32), ((2 * chunk,), F32), states, ((modes,), F32), width=broad),
        [pltpu.VMEM((chunk, broad), F32)], 8 * unit,
    )
    conv, sums, carried, moved = call(
        functools.partial(forward_kernel, chunk), grid,
        held_inputs(lam, res, parts) + inputs(conv_local) + held_inputs(gain, pieces, q, og),
        [(((length, channels), F32), (1, width), True), (((2, length), F32), None, True)]
        + outputs(states, ((modes,), F32)),
        [held, steps, pltpu.VMEM((2, length, LANES), F32)], unit, forward_begin, forward_end,
    )
    peers = lax.ppermute(sums, "chan", [(0, 1), (1, 0)])
    y_out, grad_q, gate, gain_part, gw, state = call(
        functools.partial(gate_kernel, chunk), grid,
        held_inputs(lam, gain) + [(sums, None, True), (peers, None, True)] + held_inputs(conv, q, og),
        outputs(((length,), BF16), ((length,), BF16), ((length,), F32), ((1,), F32), states, send),
        [pltpu.VMEM((length, LANES), F32)] * 2, unit, functools.partial(gate_begin, model_width),
    )
    later = lax.all_to_all(state, "ctx", 0, 0)
    rows = 2 * modes + ROWS
    grads_shape = (groups, rows, LANES)
    vg_local, grads = call(
        functools.partial(backward_kernel, chunk), grid,
        inputs(lam, gate, vals, ks, carried, moved, slopes, gw, gain_part) + basis,
        outputs(((length,), F32)) + [((grads_shape, F32), (0, width // LANES))],
        [pltpu.VMEM((chunk, width), F32)], 8 * unit,
    )
    adj, grads = call(
        functools.partial(adjoint_kernel, float(length)), 1,
        [(grads, (0, groups))] + [(a, None, True) for a in (lam, res, slope, later)],
        [((lam.shape, F32), (1, channels)), ((grads_shape, BF16), (0, groups))], [], channels * modes * 40,
    )
    grad_k, grad_v = call(
        functools.partial(finish_kernel, chunk), grid, inputs(adj) + held_inputs(lam, res) + inputs(gw, vg_local) + held_inputs(k, v),
        outputs(((length,), BF16), ((length,), BF16)), [held], unit,
    )
    both = ("ctx", "dp")
    if count * lax.axis_size("dp") == groups:
        parts = lax.all_to_all(grads, both, 0, 0)
        mine = jnp.sum(parts.astype(F32), axis=0).astype(BF16)
        total = lax.all_to_all(jnp.broadcast_to(mine[None], grads.shape), both, 0, 0).astype(F32)
    else:
        total = lax.psum(grads.astype(F32), both)
    by_mode = total.transpose(1, 0, 2).reshape(rows, channels)
    return (
        y_out[None],
        grad_q[None],
        grad_k[None],
        grad_v[None],
        by_mode[:modes].T,
        by_mode[modes : 2 * modes].T,
        by_mode[2 * modes],
    )


def solution(mesh):
    streams = P("dp", "ctx", "chan")
    in_specs = (streams,) * 4 + (P("chan"), P("chan", None), P("chan", None))
    out_specs = (streams,) * 4 + (P("chan", None), P("chan", None), P("chan"))
    return jax.shard_map(shards, mesh=mesh, in_specs=in_specs, out_specs=out_specs, check_vma=False)
```
